32 devices in a mesh: section: 4 (over z), seq: 8 (over y, x, core).
Axes of the slice: x: 2, y: 2, z: 4, core: 2. Of those that a mesh axis runs over, the one named last changes fastest.
Arguments:
- forward_input: bfloat16 [4, 1024, 1024], P('section', 'seq'), may hold values from -6 to 6
- stored_input: bfloat16 [4, 1024, 1024], P('section', 'seq'), may hold values from -6 to 6
- output_cotangent: bfloat16 [4, 1024, 1024], P('section', 'seq'), may hold values from -6 to 6
- norm_gain: float32 [4, 1024], P('section'), may hold values from 0.5 to 2
- query_weight: bfloat16 [4, 1024, 512], P('section'), may hold values from -0.325 to 0.325
- key_weight: bfloat16 [4, 1024, 128], P('section'), may hold values from -7.3125 to 7.3125
- value_weight: bfloat16 [4, 1024, 128], P('section'), may hold values from -0.1875 to 0.1875
- output_weight: bfloat16 [4, 512, 1024], P('section'), may hold values from -0.25 to 0.25
- frame_index: int32 [1024], replicated, may hold values from 0 to 3, as said below
- valid_counts: int32 [8], replicated, may hold values from 32 to 128
Outputs:
- forward_next: bfloat16 [4, 1024, 1024], P('section', 'seq')
- backward_next: bfloat16 [4, 1024, 1024], P('section', 'seq')
The draws below stay inside these ranges and needn't reach their ends.
Inputs may be any that keep to these rules, and one draw needn't show every extreme that they name: `frame_index`: frame numbers start at 0, never fall along the sequence, and every number up to the largest occurs.
All inputs are finite; a program needn't handle non-finite values.
Results may differ from the reference program's by a relative error of at most 0.028.
The reference program's roundings to bfloat16 on the way count: a program that leaves them out, or rounds other values in their place, can miss the bound.
Values may be sent and summed in bfloat16 or wider, within the bound.
No kernel may reach another device: no remote copies, remote signals or barrier semaphores. Data moves between devices by JAX's collectives and lax.ppermute only.
A program may use at most 64 MiB of HBM per device.

```python
import math
from functools import partial
import jax
import jax.numpy as jnp
from jax import lax

D = 1024
HEADS = 8
KV_HEADS = 2
HEAD_DIM = 64
SLICE_TOK = 128
SECTIONS = 4
SLICES = 8
TOKENS = 1024
FRAMES = 4


def weight_pair(base_key):
    spread = 1.3 / D ** 0.5
    query_part = spread * jnp.clip(jax.random.normal(jax.random.fold_in(base_key, 101), (SECTIONS, D, HEADS * HEAD_DIM), jnp.float32), -8.0, 8.0)
    key_part = spread * jnp.clip(jax.random.normal(jax.random.fold_in(base_key, 102), (SECTIONS, D, KV_HEADS * HEAD_DIM), jnp.float32), -8.0, 8.0)
    return (query_part, key_part)


def draw_query_weight(key, part):
    return weight_pair(key)[0].astype(jnp.bfloat16)


def draw_key_weight(key, part):
    return weight_pair(key)[1].astype(jnp.bfloat16)


def draw_frame_index(key, part):
    marks = jax.random.permutation(jax.random.fold_in(key, 201), TOKENS - 1)[:FRAMES - 1] + 1
    position = jnp.arange(TOKENS, dtype=jnp.int32)
    return jnp.sum((position[:, None] >= marks[None, :]).astype(jnp.int32), axis=1).astype(jnp.int32)


def with_ends(values, own_key, least, high):
    spot = [jax.random.randint(jax.random.fold_in(own_key, axis), (), 0, length) for axis, length in enumerate(values.shape)]
    widest = values.shape.index(max(values.shape))
    neighbour = spot[:widest] + [(spot[widest] + 1) % values.shape[widest]] + spot[widest + 1:]
    return values.at[tuple(spot)].set(least).at[tuple(neighbour)].set(high)


def levels(own_key, shape, cuts, least, largest):
    factor_of = 1.0
    for axis_at, blocks in cuts:
        draws = jax.random.uniform(jax.random.fold_in(jax.random.fold_in(own_key, 6), axis_at), (blocks,), jnp.float32, least / len(cuts), largest / len(cuts))
        factor_of = factor_of * jnp.repeat(jnp.exp(draws), shape[axis_at] // blocks).reshape((-1,) + (1,) * (len(shape) - 1 - axis_at))
    return factor_of


def bell_draw(stream_key, shape, scale, most, pieces=(), kind=jnp.bfloat16):
    factor_of = levels(stream_key, shape, pieces, -0.22, 0.18) if pieces else 1.0
    array = jax.random.normal(stream_key, shape, jnp.float32) * scale * factor_of
    return jnp.minimum(jnp.maximum(array, -most), most).astype(kind)


def setup_inputs(seed: int = 0) -> dict:
    seeds = jax.random.split(jax.random.key(seed), 11)
    forward_input = bell_draw(seeds[0], (SECTIONS, TOKENS, D), 1.0, 6.0, ((0, 4), (1, 8)))
    stored_input = bell_draw(seeds[1], (SECTIONS, TOKENS, D), 1.0, 6.0, ((0, 4), (1, 8)))
    output_cotangent = bell_draw(seeds[2], (SECTIONS, TOKENS, D), 1.0, 6.0, ((0, 4), (1, 8)))
    norm_gain = jnp.clip(jnp.exp(math.log(2.0) - 1.3862944 * jax.random.uniform(seeds[3], (SECTIONS, D), jnp.float32) ** levels(seeds[3], (SECTIONS, D), ((0, 4),), -0.2, 0.2)), 0.5, 2.0)
    query_weight = draw_query_weight(jax.random.fold_in(seeds[10], 71), 0)
    key_weight = draw_key_weight(jax.random.fold_in(seeds[10], 71), 0)
    value_weight = bell_draw(seeds[6], (SECTIONS, D, KV_HEADS * HEAD_DIM), D ** -0.5, 0.1875, ((0, 4),))
    output_weight = bell_draw(seeds[7], (SECTIONS, HEADS * HEAD_DIM, D), (HEADS * HEAD_DIM) ** -0.5, 0.25, ((0, 4),))
    frame_index = draw_frame_index(jax.random.fold_in(seeds[10], 71), 0)
    valid_counts = with_ends(jax.random.randint(seeds[9], (SLICES,), SLICE_TOK // 4, SLICE_TOK + 1), jax.random.fold_in(seeds[9], 1), SLICE_TOK // 4, SLICE_TOK).astype(jnp.int32)
    return {"forward_input": forward_input, "stored_input": stored_input, "output_cotangent": output_cotangent, "norm_gain": norm_gain, "query_weight": query_weight, "key_weight": key_weight, "value_weight": value_weight, "output_weight": output_weight, "frame_index": frame_index, "valid_counts": valid_counts}


NORM_EPSILON = 1e-05
MASKED_SCORE = -1e+30

def normalize(inputs, norm_scale):
    widened = inputs.astype(jnp.float32)
    inverse = lax.rsqrt(lax.optimization_barrier(jnp.mean(widened * widened, axis=-1, keepdims=True)) + NORM_EPSILON)
    return ((widened * inverse * norm_scale).astype(jnp.bfloat16), inverse)

def project(normed, weight):
    return jnp.dot(normed, weight, preferred_element_type=jnp.float32).astype(jnp.bfloat16)

def visibility(frame_index, valid_counts):
    inside = jnp.arange(SLICE_TOK, dtype=jnp.int32)
    valid_flags = (inside[None, :] < valid_counts[:, None]).reshape(TOKENS)
    return valid_flags[None, :] & (frame_index[None, :] <= frame_index[:, None])

def heads_first(matrix, head_count):
    return matrix.reshape(TOKENS, head_count, HEAD_DIM).transpose(1, 0, 2)

def shared_heads(matrix):
    return jnp.repeat(heads_first(matrix, KV_HEADS), HEADS // KV_HEADS, axis=0)

def head_forward(visible, operands):
    query_head, key_head, value_head = operands
    score_scale = 1.0 / math.sqrt(HEAD_DIM)
    scores = jnp.dot(query_head, key_head.T, preferred_element_type=jnp.float32) * score_scale
    scores = jnp.where(visible, scores, MASKED_SCORE)
    row_max = lax.optimization_barrier(jnp.max(scores, axis=1, keepdims=True))
    weights = jnp.where(visible, jnp.exp(scores - row_max), 0.0)
    row_sum = lax.optimization_barrier(jnp.sum(weights, axis=1, keepdims=True))
    attended = jnp.dot(weights.astype(jnp.bfloat16), value_head, preferred_element_type=jnp.float32) / row_sum
    return (attended.astype(jnp.bfloat16), (row_max + jnp.log(row_sum))[:, 0])

def head_backward(visible, operands):
    query_head, key_head, value_head, dout_head, log_sum, delta = operands
    score_scale = 1.0 / math.sqrt(HEAD_DIM)
    scores = jnp.dot(query_head, key_head.T, preferred_element_type=jnp.float32) * score_scale
    scores = jnp.where(visible, scores, MASKED_SCORE)
    probability = jnp.where(visible, jnp.exp(scores - log_sum[:, None]), 0.0)
    prob_grads = jnp.dot(dout_head, value_head.T, preferred_element_type=jnp.float32)
    score_grads = (probability * (prob_grads - delta[:, None])).astype(jnp.bfloat16)
    query_grad = jnp.dot(score_grads, key_head, preferred_element_type=jnp.float32) * score_scale
    key_grad = jnp.dot(score_grads.T, query_head, preferred_element_type=jnp.float32) * score_scale
    value_grad = jnp.dot(probability.astype(jnp.bfloat16).T, dout_head, preferred_element_type=jnp.float32)
    return (query_grad.astype(jnp.bfloat16), key_grad, value_grad)

def forward_layer(inputs, norm_scale, query_proj, key_proj, value_proj, out_proj, visible):
    normed, inverse = normalize(inputs, norm_scale)
    queries = project(normed, query_proj)
    keys = project(normed, key_proj)
    values = project(normed, value_proj)
    heads_out, log_sums = lax.map(partial(head_forward, visible), (heads_first(queries, HEADS), shared_heads(keys), shared_heads(values)))
    attended = heads_out.transpose(1, 0, 2).reshape(TOKENS, HEADS * HEAD_DIM)
    layer_out = inputs.astype(jnp.float32) + jnp.dot(attended, out_proj, preferred_element_type=jnp.float32)
    return (layer_out.astype(jnp.bfloat16), inverse, queries, keys, values, attended, log_sums)

def backward_layer(inputs, cotangent, norm_scale, query_proj, key_proj, value_proj, out_proj, visible):
    _, inverse, queries, keys, values, attended, log_sums = forward_layer(inputs, norm_scale, query_proj, key_proj, value_proj, out_proj, visible)
    dout = jnp.dot(cotangent, out_proj.T, preferred_element_type=jnp.float32).astype(jnp.bfloat16)
    deltas = lax.optimization_barrier(jnp.sum((dout.astype(jnp.float32) * attended.astype(jnp.float32)).reshape(TOKENS, HEADS, HEAD_DIM), axis=-1)).T
    query_grad, key_grad, value_grad = lax.map(partial(head_backward, visible), (heads_first(queries, HEADS), shared_heads(keys), shared_heads(values), heads_first(dout, HEADS), log_sums, deltas))
    group_size = HEADS // KV_HEADS
    query_grad = query_grad.transpose(1, 0, 2).reshape(TOKENS, HEADS * HEAD_DIM)
    key_grad = key_grad.reshape(KV_HEADS, group_size, TOKENS, HEAD_DIM).sum(axis=1).transpose(1, 0, 2).reshape(TOKENS, KV_HEADS * HEAD_DIM).astype(jnp.bfloat16)
    value_grad = value_grad.reshape(KV_HEADS, group_size, TOKENS, HEAD_DIM).sum(axis=1).transpose(1, 0, 2).reshape(TOKENS, KV_HEADS * HEAD_DIM).astype(jnp.bfloat16)
    normed_grad = jnp.dot(query_grad, query_proj.T, preferred_element_type=jnp.float32)
    normed_grad = normed_grad + jnp.dot(key_grad, key_proj.T, preferred_element_type=jnp.float32)
    normed_grad = normed_grad + jnp.dot(value_grad, value_proj.T, preferred_element_type=jnp.float32)
    scaled_grad = normed_grad * norm_scale
    widened = inputs.astype(jnp.float32)
    input_grad = cotangent.astype(jnp.float32) + inverse * scaled_grad - widened * inverse ** 3 * lax.optimization_barrier(jnp.mean(widened * scaled_grad, axis=-1, keepdims=True))
    return input_grad.astype(jnp.bfloat16)

def reference(forward_input, stored_input, output_cotangent, norm_gain, query_weight, key_weight, value_weight, output_weight, frame_index, valid_counts):
    visible = visibility(frame_index, valid_counts)

    def one_section(operands):
        fwd_inputs, bwd_inputs, cotangent, norm_scale, query_proj, key_proj, value_proj, out_proj = operands
        layer_out = forward_layer(fwd_inputs, norm_scale, query_proj, key_proj, value_proj, out_proj, visible)[0]
        input_grad = backward_layer(bwd_inputs, cotangent, norm_scale, query_proj, key_proj, value_proj, out_proj, visible)
        return (layer_out, input_grad)
    layer_out, input_grad = lax.map(one_section, (forward_input, stored_input, output_cotangent, norm_gain, query_weight, key_weight, value_weight, output_weight))
    return (jnp.roll(layer_out, 1, axis=0), jnp.roll(input_grad, -1, axis=0))
```

```python
from functools import partial
import math

import jax
import jax.numpy as jnp
from jax import lax
from jax.experimental import pallas as pl
from jax.experimental.pallas import tpu as pltpu
from jax.sharding import PartitionSpec as P

HEADS = 8
KV_HEADS = 2
HEAD_DIM = 64
GROUP = HEADS // KV_HEADS
KV_COLS = KV_HEADS * HEAD_DIM
PAIRS = HEADS // 2

NORM_EPSILON = 1e-05
MASKED_SCORE = -1e30
F32 = jnp.float32
BF16 = jnp.bfloat16

NN = (((1,), (0,)), ((), ()))
NT = (((1,), (1,)), ((), ()))


def dot(a, b, dims=NN):
    return lax.dot_general(a, b, dims, preferred_element_type=F32)


def vmem(count):
    return [pl.BlockSpec(memory_space=pltpu.VMEM)] * count


def shape(dims, dtype):
    return jax.ShapeDtypeStruct(dims, dtype)


def rms(inputs, gain):
    widened = inputs.astype(F32)
    inverse = lax.rsqrt(jnp.mean(widened * widened, axis=-1, keepdims=True) + NORM_EPSILON)
    return (widened * inverse * gain).astype(BF16), inverse, widened


def project_kv(x_ref, gain_ref, wk_ref, wv_ref, kv_ref):
    normed, _, _ = rms(x_ref[...], gain_ref[...])
    kv_ref[:, :KV_COLS] = dot(normed, wk_ref[...]).astype(BF16)
    kv_ref[:, KV_COLS:] = dot(normed, wv_ref[...]).astype(BF16)


def spread_heads(flat, out_ref, scale):
    rows = flat.shape[0]
    flat = flat.astype(BF16).astype(F32) * scale
    lane = lax.broadcasted_iota(jnp.int32, (rows, KV_COLS), 1)
    for head in range(HEADS):
        tile = head // 2
        block = flat[:, tile * KV_COLS : (tile + 1) * KV_COLS]
        group = head // GROUP
        if head % 2 != group:
            block = pltpu.roll(block, HEAD_DIM, 1)
        block = jnp.where((lane // HEAD_DIM) == group, block, 0.0)
        out_ref[head * rows : (head + 1) * rows, :] = block.astype(BF16)


def prepare(
    order,
    me_ref,
    counts_ref,
    xf_ref,
    xb_ref,
    cot_ref,
    gain_ref,
    wq_ref,
    wk_ref,
    wv_ref,
    wo_ref,
    frames_ref,
    kvf_ref,
    qf_ref,
    qb_ref,
    dout_ref,
    bias_ref,
):
    gain = gain_ref[...]
    rows = xf_ref.shape[0]
    normed_f, _, _ = rms(xf_ref[...], gain)
    kvf_ref[:, :KV_COLS] = dot(normed_f, wk_ref[...]).astype(BF16)
    kvf_ref[:, KV_COLS:] = dot(normed_f, wv_ref[...]).astype(BF16)
    scale = 1.0 / math.sqrt(HEAD_DIM)
    spread_heads(dot(normed_f, wq_ref[...]), qf_ref, scale)
    normed_b, _, _ = rms(xb_ref[...], gain)
    spread_heads(dot(normed_b, wq_ref[...]), qb_ref, scale)
    spread_heads(dot(cot_ref[...], wo_ref[...], NT), dout_ref, 1.0)
    me = me_ref[0]
    row = lax.broadcasted_iota(jnp.int32, (rows, rows), 0)
    query_frames = jnp.broadcast_to(frames_ref[pl.ds(me, 1), :], (rows, rows))
    for place, step in enumerate(order):
        source = jnp.bitwise_xor(me, step)
        own = jnp.broadcast_to(frames_ref[pl.ds(source, 1), :], (rows, rows))
        key_frames = jnp.transpose(own.astype(F32)).astype(jnp.int32)
        visible = (key_frames <= query_frames) & (row < counts_ref[source])
        bias_ref[place * rows : (place + 1) * rows, :] = jnp.where(visible, 0.0, MASKED_SCORE)


def scores_of(keys_ref, q_rows, bias_ref, s_ref, chunk):
    total = keys_ref.shape[0]
    top = None
    for first in range(0, total, chunk):
        block = dot(keys_ref[first : first + chunk, :KV_COLS], q_rows, NT)
        bias = bias_ref[first : first + chunk, :]
        block = block + jnp.concatenate([bias, bias], axis=1)
        s_ref[first : first + chunk, :] = block
        part = jnp.max(block, axis=0, keepdims=True)
        top = part if top is None else jnp.maximum(top, part)
    return top


def attend_backward(count, *refs):
    pieces = refs[:count]
    q_ref, dout_ref, bias_ref = refs[count : count + 3]
    even_refs = refs[count + 3 : count + 3 + count // 2]
    odd_ref, dq_ref = refs[count + 3 + count // 2 : count + 5 + count // 2]
    kv_ref, s_ref, dp_ref, e_ref, u_ref, rs_ref, dqt_ref, qs_ref, ds_ref = refs[count + 5 + count // 2 :]
    rows = pieces[0].shape[0]
    total = rows * count
    chunk = 2 * rows
    for place, piece in enumerate(pieces):
        kv_ref[place * rows : (place + 1) * rows, :] = piece[...]
    keys_t = jnp.transpose(kv_ref[:, :KV_COLS])
    scale = 1.0 / math.sqrt(HEAD_DIM)
    wide = 2 * rows
    for pair in range(PAIRS):
        cols = slice(pair * wide, (pair + 1) * wide)
        q_rows = q_ref[cols, :]
        dout_rows = dout_ref[cols, :]
        top = scores_of(kv_ref, q_rows, bias_ref, s_ref, chunk)
        row_sum = jnp.zeros((1, wide), F32)
        mixed = jnp.zeros((1, wide), F32)
        for first in range(0, total, chunk):
            weights = jnp.exp(s_ref[first : first + chunk, :] - top)
            prob_grad = dot(kv_ref[first : first + chunk, KV_COLS:], dout_rows, NT)
            row_sum = row_sum + jnp.sum(weights, axis=0, keepdims=True)
            mixed = mixed + jnp.sum(weights * prob_grad, axis=0, keepdims=True)
            dp_ref[first : first + chunk, :] = prob_grad
            s_ref[first : first + chunk, :] = weights
        inverse_sum = 1.0 / row_sum
        delta = mixed * inverse_sum
        rs_ref[2 * pair : 2 * pair + 1, :] = inverse_sum[:, :rows]
        rs_ref[2 * pair + 1 : 2 * pair + 2, :] = inverse_sum[:, rows:]
        for first in range(0, total, chunk):
            weights = s_ref[first : first + chunk, :]
            e_ref[first : first + chunk, cols] = weights.astype(BF16)
            u_ref[first : first + chunk, cols] = (
                weights * (dp_ref[first : first + chunk, :] - delta)
            ).astype(BF16)
        query_grad = dot(keys_t, u_ref[:, cols]) * (inverse_sum * scale)
        group = (2 * pair) // GROUP
        part = query_grad[group * HEAD_DIM : (group + 1) * HEAD_DIM, :]
        dqt_ref[2 * pair * HEAD_DIM : (2 * pair + 1) * HEAD_DIM, :] = part[:, :rows]
        dqt_ref[(2 * pair + 1) * HEAD_DIM : (2 * pair + 2) * HEAD_DIM, :] = part[:, rows:]
    dq_ref[...] = jnp.transpose(dqt_ref[...]).astype(BF16)
    rs_t = jnp.transpose(rs_ref[...])
    for head in range(HEADS):
        lines = slice(head * rows, (head + 1) * rows)
        factor = rs_t[:, head : head + 1]
        qs_ref[lines, :] = (q_ref[lines, :].astype(F32) * factor).astype(BF16)
        ds_ref[lines, :] = (dout_ref[lines, :].astype(F32) * factor).astype(BF16)
    q_scaled = qs_ref[...]
    dout_scaled = ds_ref[...]
    for place in range(count):
        lines = slice(place * rows, (place + 1) * rows)
        key_grad = dot(u_ref[lines, :], q_scaled).astype(BF16)
        value_grad = dot(e_ref[lines, :], dout_scaled).astype(BF16)
        half = count // 2
        target = even_refs[place] if place < half else odd_ref.at[place - half]
        target[:, :KV_COLS] = key_grad
        target[:, KV_COLS:] = value_grad


def attend_forward(count, *refs):
    pieces = refs[:count]
    q_ref, bias_ref, x_ref, wo_ref, out_ref = refs[count : count + 5]
    kv_ref, s_ref, e_ref, at_ref = refs[count + 5 :]
    rows = pieces[0].shape[0]
    total = rows * count
    chunk = 2 * rows
    for place, piece in enumerate(pieces):
        kv_ref[place * rows : (place + 1) * rows, :] = piece[...]
    values_t = jnp.transpose(kv_ref[:, KV_COLS:])
    wide = 2 * rows
    for pair in range(PAIRS):
        q_rows = q_ref[pair * wide : (pair + 1) * wide, :]
        top = scores_of(kv_ref, q_rows, bias_ref, s_ref, chunk)
        row_sum = jnp.zeros((1, wide), F32)
        for first in range(0, total, chunk):
            weights = jnp.exp(s_ref[first : first + chunk, :] - top)
            row_sum = row_sum + jnp.sum(weights, axis=0, keepdims=True)
            e_ref[first : first + chunk, :] = weights.astype(BF16)
        mixed = dot(values_t, e_ref[...]) * (1.0 / row_sum)
        group = (2 * pair) // GROUP
        part = mixed[group * HEAD_DIM : (group + 1) * HEAD_DIM, :]
        at_ref[2 * pair * HEAD_DIM : (2 * pair + 1) * HEAD_DIM, :] = part[:, :rows]
        at_ref[(2 * pair + 1) * HEAD_DIM : (2 * pair + 2) * HEAD_DIM, :] = part[:, rows:]
    attended = jnp.transpose(at_ref[...]).astype(BF16)
    out_ref[...] = (x_ref[...].astype(F32) + dot(attended, wo_ref[...])).astype(BF16)


def query_back(dq_ref, wq_ref, out_ref):
    out_ref[...] = dot(dq_ref[...], wq_ref[...], NT)


def add_pieces(count, *refs):
    for place in range(count):
        left = refs[place][...].astype(F32)
        refs[count + 1 + place][...] = (left + refs[count][place].astype(F32)).astype(BF16)


def input_back(count, *refs):
    pieces = refs[:count]
    base_ref, x_ref, cot_ref, gain_ref, wk_ref, wv_ref, out_ref = refs[count:]
    grads = pieces[0][...].astype(F32)
    for piece in pieces[1:]:
        grads = grads + piece[...].astype(F32)
    grads = grads.astype(BF16)
    gain = gain_ref[...]
    normed_grad = base_ref[...] + dot(grads[:, :KV_COLS], wk_ref[...], NT)
    normed_grad = normed_grad + dot(grads[:, KV_COLS:], wv_ref[...], NT)
    _, inverse, widened = rms(x_ref[...], gain)
    scaled = normed_grad * gain
    mean = jnp.mean(widened * scaled, axis=-1, keepdims=True)
    grad = cot_ref[...].astype(F32) + inverse * scaled - widened * (inverse * inverse * inverse * mean)
    out_ref[...] = grad.astype(BF16)


def call(kernel, outs, args, scratch=(), smem=0, name=None):
    specs = [pl.BlockSpec(memory_space=pltpu.SMEM)] * smem + vmem(len(args) - smem)
    out_specs = vmem(len(outs)) if isinstance(outs, (list, tuple)) else vmem(1)[0]
    return pl.pallas_call(
        kernel, out_shape=outs, in_specs=specs, out_specs=out_specs, scratch_shapes=list(scratch), name=name
    )(*args)


def swap(block, step, size):
    return lax.ppermute(block, "seq", [(i, i ^ step) for i in range(size)])


def gather_pieces(block, size):
    if size > 8 or size % 2:
        everything = lax.all_gather(block, "seq", axis=0)
        me = lax.axis_index("seq")
        return [lax.dynamic_index_in_dim(everything, me ^ step, 0, False) for step in order_of(size)]
    near = [block] + [swap(block, step, size) for step in range(2, size, 2)]
    return near + [swap(piece, 1, size) for piece in near]


def order_of(size):
    return list(range(0, size, 2)) + list(range(1, size, 2))


def on_device(
    size,
    forward_input,
    stored_input,
    output_cotangent,
    norm_gain,
    query_weight,
    key_weight,
    value_weight,
    output_weight,
    frame_index,
    valid_counts,
):
    xf, xb, cot = forward_input[0], stored_input[0], output_cotangent[0]
    wq, wk, wv, wo = query_weight[0], key_weight[0], value_weight[0], output_weight[0]
    rows, width = xf.shape
    total = rows * size
    sections = lax.axis_size("section")
    order = order_of(size)
    half = size // 2
    kv_shape = shape((rows, 2 * KV_COLS), BF16)
    spread = shape((HEADS * rows, KV_COLS), BF16)
    wide = 2 * rows

    kvb = call(project_kv, kv_shape, (xb, norm_gain, wk, wv), name="project_kv")
    pieces_b = gather_pieces(kvb, size)
    me = lax.axis_index("seq").astype(jnp.int32).reshape(1)
    kvf, qf, qb, dout, bias = call(
        partial(prepare, order),
        (kv_shape, spread, spread, spread, shape((total, rows), F32)),
        (me, valid_counts, xf, xb, cot, norm_gain, wq, wk, wv, wo, frame_index.reshape(size, rows)),
        smem=2,
        name="prepare",
    )
    pieces_f = gather_pieces(kvf, size)
    *grads, dq = call(
        partial(attend_backward, size),
        (kv_shape,) * half + (shape((half, rows, 2 * KV_COLS), BF16), shape((rows, HEADS * HEAD_DIM), BF16)),
        (*pieces_b, qb, dout, bias),
        scratch=(
            pltpu.VMEM((total, 2 * KV_COLS), BF16),
            pltpu.VMEM((total, wide), F32),
            pltpu.VMEM((total, wide), F32),
            pltpu.VMEM((total, HEADS * rows), BF16),
            pltpu.VMEM((total, HEADS * rows), BF16),
            pltpu.VMEM((HEADS, rows), F32),
            pltpu.VMEM((HEADS * HEAD_DIM, rows), F32),
            pltpu.VMEM((HEADS * rows, KV_COLS), BF16),
            pltpu.VMEM((HEADS * rows, KV_COLS), BF16),
        ),
        name="attend_backward",
    )
    even, odd = grads[:half], grads[half]
    if size > 8 or size % 2:
        index = lax.axis_index("seq")
        both = jnp.stack(list(even) + [odd[i] for i in range(half)]).astype(F32)
        places = jnp.argsort(jnp.array(order, jnp.int32) ^ index)
        summed = lax.psum_scatter(both[places], "seq", scatter_dimension=0, tiled=True)
        received = [summed[0].astype(BF16)]
    else:
        other = swap(odd, 1, size)
        sums = call(partial(add_pieces, half), (kv_shape,) * half, (*even, other), name="add_pieces")
        received = [sums[0]] + [swap(sums[i], 2 * i, size) for i in range(1, half)]
    layer_out = call(
        partial(attend_forward, size),
        shape((rows, width), BF16),
        (*pieces_f, qf, bias, xf, wo),
        scratch=(
            pltpu.VMEM((total, 2 * KV_COLS), BF16),
            pltpu.VMEM((total, wide), F32),
            pltpu.VMEM((total, wide), BF16),
            pltpu.VMEM((HEADS * HEAD_DIM, rows), F32),
        ),
        name="attend_forward",
    )
    forward_next = lax.ppermute(layer_out, "section", [((i - 1) % sections, i) for i in range(sections)])
    base = call(query_back, shape((rows, width), F32), (dq, wq), name="query_back")
    input_grad = call(
        partial(input_back, len(received)),
        shape((rows, width), BF16),
        (*received, base, xb, cot, norm_gain, wk, wv),
        name="input_back",
    )
    backward_next = lax.ppermute(input_grad, "section", [((i + 1) % sections, i) for i in range(sections)])
    return (forward_next[None], backward_next[None])


def solution(mesh):
    return jax.shard_map(
        partial(on_device, mesh.shape["seq"]),
        mesh=mesh,
        in_specs=(
            P("section", "seq", None),
            P("section", "seq", None),
            P("section", "seq", None),
            P("section", None),
            P("section", None, None),
            P("section", None, None),
            P("section", None, None),
            P("section", None, None),
            P(),
            P(),
        ),
        out_specs=(P("section", "seq", None), P("section", "seq", None)),
        check_vma=False,
    )
```

```python
from functools import partial
import math

import jax
import jax.numpy as jnp
from jax import lax
from jax.experimental import pallas as pl
from jax.experimental.pallas import tpu as pltpu
from jax.sharding import PartitionSpec as P


HEADS = 8
KV_HEADS = 2
HEAD_DIM = 64
GROUP = HEADS // KV_HEADS
KV_COLS = KV_HEADS * HEAD_DIM
PAIRS = HEADS // 2

NORM_EPSILON = 1e-05
MASKED_SCORE = -1e30

F32 = jnp.float32
BF16 = jnp.bfloat16

NN = (((1,), (0,)), ((), ()))
NT = (((1,), (1,)), ((), ()))


def dot(a, b, dims=NN):
    return lax.dot_general(a, b, dims, preferred_element_type=F32)


def vmem(count):
    return [pl.BlockSpec(memory_space=pltpu.VMEM)] * count


def shape(dims, dtype):
    return jax.ShapeDtypeStruct(dims, dtype)


def rms(inputs, gain):
    widened = inputs.astype(F32)
    inverse = lax.rsqrt(jnp.mean(widened * widened, axis=-1, keepdims=True) + NORM_EPSILON)
    return (widened * inverse * gain).astype(BF16), inverse, widened


def project_kv(gain_ref, xf_hbm, xb_hbm, wk_hbm, wv_hbm, kv_ref, xf_ref, xb_ref, wk_ref, wv_ref, sems):
    copies = [
        pltpu.make_async_copy(source, target, sems.at[place])
        for place, (source, target) in enumerate(
            ((xf_hbm, xf_ref), (wk_hbm, wk_ref), (wv_hbm, wv_ref), (xb_hbm, xb_ref))
        )
    ]
    for copy in copies:
        copy.start()
    gain = gain_ref[...]
    rows = xf_ref.shape[0]
    copies[0].wait()
    normed_f, _, _ = rms(xf_ref[...], gain)
    copies[3].wait()
    normed_b, _, _ = rms(xb_ref[...], gain)
    normed = jnp.concatenate([normed_f, normed_b], axis=0)
    copies[1].wait()
    copies[2].wait()
    for place, weight_ref in enumerate((wk_ref, wv_ref)):
        both = dot(normed, weight_ref[...]).astype(BF16)
        kv_ref[:, place * KV_COLS : (place + 1) * KV_COLS] = both[:rows]
        kv_ref[:, (2 + place) * KV_COLS : (3 + place) * KV_COLS] = both[rows:]


def spread_heads(flat, out_ref, scale):
    rows = flat.shape[0]
    flat = flat.astype(BF16).astype(F32) * scale
    lane = lax.broadcasted_iota(jnp.int32, (rows, KV_COLS), 1)
    for head in range(HEADS):
        tile = head // 2
        block = flat[:, tile * KV_COLS : (tile + 1) * KV_COLS]
        group = head // GROUP
        if head % 2 != group:
            block = pltpu.roll(block, HEAD_DIM, 1)
        block = jnp.where((lane // HEAD_DIM) == group, block, 0.0)
        out_ref[head * rows : (head + 1) * rows, :] = block.astype(BF16)


def prepare(
    order,
    me_ref,
    counts_ref,
    xf_ref,
    xb_ref,
    gain_ref,
    frames_ref,
    cot_hbm,
    wq_hbm,
    wo_hbm,
    qf_ref,
    qb_ref,
    dout_ref,
    bias_ref,
    cot_ref,
    wq_ref,
    wo_ref,
    sems,
):
    copies = [
        pltpu.make_async_copy(source, target, sems.at[place])
        for place, (source, target) in enumerate(((wq_hbm, wq_ref), (cot_hbm, cot_ref), (wo_hbm, wo_ref)))
    ]
    for copy in copies:
        copy.start()
    gain = gain_ref[...]
    rows = xf_ref.shape[0]
    me = me_ref[0]
    row = lax.broadcasted_iota(jnp.int32, (rows, rows), 0)
    query_frames = jnp.broadcast_to(frames_ref[pl.ds(me, 1), :], (rows, rows))
    for place, step in enumerate(order):
        source = jnp.bitwise_xor(me, step)
        own = jnp.broadcast_to(frames_ref[pl.ds(source, 1), :], (rows, rows))
        key_frames = jnp.transpose(own.astype(F32)).astype(jnp.int32)
        visible = (key_frames <= query_frames) & (row < counts_ref[source])
        bias_ref[place * rows : (place + 1) * rows, :] = jnp.where(visible, 0.0, MASKED_SCORE)
    normed_f, _, _ = rms(xf_ref[...], gain)
    normed_b, _, _ = rms(xb_ref[...], gain)
    scale = 1.0 / math.sqrt(HEAD_DIM)
    copies[0].wait()
    queries = dot(jnp.concatenate([normed_f, normed_b], axis=0), wq_ref[...])
    spread_heads(queries[:rows], qf_ref, scale)
    spread_heads(queries[rows:], qb_ref, scale)
    copies[1].wait()
    copies[2].wait()
    spread_heads(dot(cot_ref[...], wo_ref[...], NT), dout_ref, 1.0)


def scores_of(keys_ref, q_rows, bias_ref, s_ref, chunk):
    total = keys_ref.shape[0]
    top = None
    for first in range(0, total, chunk):
        block = dot(keys_ref[first : first + chunk, :KV_COLS], q_rows, NT)
        bias = bias_ref[first : first + chunk, :]
        block = block + jnp.concatenate([bias, bias], axis=1)
        s_ref[first : first + chunk, :] = block
        part = jnp.max(block, axis=0, keepdims=True)
        top = part if top is None else jnp.maximum(top, part)
    return top


def attend_backward(count, *refs):
    pieces = refs[:count]
    q_ref, dout_ref, bias_ref = refs[count : count + 3]
    even_refs = refs[count + 3 : count + 3 + count // 2]
    odd_ref, dq_ref = refs[count + 3 + count // 2 : count + 5 + count // 2]
    kv_ref, s_ref, dp_ref, e_ref, u_ref, rs_ref, dqt_ref, qs_ref, ds_ref = refs[count + 5 + count // 2 :]
    rows = pieces[0].shape[0]
    total = rows * count
    chunk = 2 * rows
    for place, piece in enumerate(pieces):
        kv_ref[place * rows : (place + 1) * rows, :] = piece[:, 2 * KV_COLS :]
    keys_t = jnp.transpose(kv_ref[:, :KV_COLS])
    scale = 1.0 / math.sqrt(HEAD_DIM)
    wide = 2 * rows
    for pair in range(PAIRS):
        cols = slice(pair * wide, (pair + 1) * wide)
        q_rows = q_ref[cols, :]
        dout_rows = dout_ref[cols, :]
        top = scores_of(kv_ref, q_rows, bias_ref, s_ref, chunk)
        row_sum = jnp.zeros((1, wide), F32)
        mixed = jnp.zeros((1, wide), F32)
        for first in range(0, total, chunk):
            weights = jnp.exp(s_ref[first : first + chunk, :] - top)
            prob_grad = dot(kv_ref[first : first + chunk, KV_COLS:], dout_rows, NT)
            row_sum = row_sum + jnp.sum(weights, axis=0, keepdims=True)
            mixed = mixed + jnp.sum(weights * prob_grad, axis=0, keepdims=True)
            dp_ref[first : first + chunk, :] = prob_grad
            s_ref[first : first + chunk, :] = weights
        inverse_sum = 1.0 / row_sum
        delta = mixed * inverse_sum
        rs_ref[2 * pair : 2 * pair + 1, :] = inverse_sum[:, :rows]
        rs_ref[2 * pair + 1 : 2 * pair + 2, :] = inverse_sum[:, rows:]
        for first in range(0, total, chunk):
            weights = s_ref[first : first + chunk, :]
            e_ref[first : first + chunk, cols] = weights.astype(BF16)
            u_ref[first : first + chunk, cols] = (
                weights * (dp_ref[first : first + chunk, :] - delta)
            ).astype(BF16)
        query_grad = dot(keys_t, u_ref[:, cols]) * (inverse_sum * scale)
        group = (2 * pair) // GROUP
        part = query_grad[group * HEAD_DIM : (group + 1) * HEAD_DIM, :]
        dqt_ref[2 * pair * HEAD_DIM : (2 * pair + 1) * HEAD_DIM, :] = part[:, :rows]
        dqt_ref[(2 * pair + 1) * HEAD_DIM : (2 * pair + 2) * HEAD_DIM, :] = part[:, rows:]
    dq_ref[...] = jnp.transpose(dqt_ref[...]).astype(BF16)
    rs_t = jnp.transpose(rs_ref[...])
    for head in range(HEADS):
        lines = slice(head * rows, (head + 1) * rows)
        factor = rs_t[:, head : head + 1]
        qs_ref[lines, :] = (q_ref[lines, :].astype(F32) * factor).astype(BF16)
        ds_ref[lines, :] = (dout_ref[lines, :].astype(F32) * factor).astype(BF16)
    q_scaled = qs_ref[...]
    dout_scaled = ds_ref[...]
    for place in range(count):
        lines = slice(place * rows, (place + 1) * rows)
        key_grad = dot(u_ref[lines, :], q_scaled).astype(BF16)
        value_grad = dot(e_ref[lines, :], dout_scaled).astype(BF16)
        half = count // 2
        target = even_refs[place] if place < half else odd_ref.at[place - half]
        target[:, :KV_COLS] = key_grad
        target[:, KV_COLS:] = value_grad


def attend_forward(count, *refs):
    pieces = refs[:count]
    q_ref, bias_ref, x_ref, wo_ref, out_ref = refs[count : count + 5]
    kv_ref, s_ref, e_ref, at_ref = refs[count + 5 :]
    rows = pieces[0].shape[0]
    total = rows * count
    chunk = 2 * rows
    for place, piece in enumerate(pieces):
        kv_ref[place * rows : (place + 1) * rows, :] = piece[:, : 2 * KV_COLS]
    values_t = jnp.transpose(kv_ref[:, KV_COLS:])
    wide = 2 * rows
    for pair in range(PAIRS):
        q_rows = q_ref[pair * wide : (pair + 1) * wide, :]
        top = scores_of(kv_ref, q_rows, bias_ref, s_ref, chunk)
        row_sum = jnp.zeros((1, wide), F32)
        for first in range(0, total, chunk):
            weights = jnp.exp(s_ref[first : first + chunk, :] - top)
            row_sum = row_sum + jnp.sum(weights, axis=0, keepdims=True)
            e_ref[first : first + chunk, :] = weights.astype(BF16)
        mixed = dot(values_t, e_ref[...]) * (1.0 / row_sum)
        group = (2 * pair) // GROUP
        part = mixed[group * HEAD_DIM : (group + 1) * HEAD_DIM, :]
        at_ref[2 * pair * HEAD_DIM : (2 * pair + 1) * HEAD_DIM, :] = part[:, :rows]
        at_ref[(2 * pair + 1) * HEAD_DIM : (2 * pair + 2) * HEAD_DIM, :] = part[:, rows:]
    attended = jnp.transpose(at_ref[...]).astype(BF16)
    out_ref[...] = (x_ref[...].astype(F32) + dot(attended, wo_ref[...])).astype(BF16)


def query_back(dq_ref, wq_ref, next_ref, out_ref, next_hbm, sem):
    copy = pltpu.make_async_copy(next_ref, next_hbm, sem)
    copy.start()
    out_ref[...] = dot(dq_ref[...], wq_ref[...], NT)
    copy.wait()


def add_pieces(count, *refs):
    for place in range(count):
        left = refs[place][...].astype(F32)
        refs[count + 1 + place][...] = (left + refs[count][place].astype(F32)).astype(BF16)


def input_back(count, *refs):
    pieces = refs[:count]
    base_ref, x_ref, cot_ref, gain_ref, wk_ref, wv_ref, out_ref = refs[count:]
    grads = pieces[0][...].astype(F32)
    for piece in pieces[1:]:
        grads = grads + piece[...].astype(F32)
    grads = grads.astype(BF16)
    gain = gain_ref[...]
    normed_grad = base_ref[...] + dot(grads[:, :KV_COLS], wk_ref[...], NT)
    normed_grad = normed_grad + dot(grads[:, KV_COLS:], wv_ref[...], NT)
    _, inverse, widened = rms(x_ref[...], gain)
    scaled = normed_grad * gain
    mean = jnp.mean(widened * scaled, axis=-1, keepdims=True)
    grad = cot_ref[...].astype(F32) + inverse * scaled - widened * (inverse * inverse * inverse * mean)
    out_ref[...] = grad.astype(BF16)


def local(array):
    return pltpu.with_memory_space_constraint(array, pltpu.VMEM)


def size_of(item):
    return math.prod(item.shape) * jnp.dtype(item.dtype).itemsize


def call(kernel, outs, args, scratch=(), sems=None, smem=0, hbm=0, out_hbm=0):
    many = isinstance(outs, (list, tuple))
    outs = list(outs) if many else [outs]
    inside, kept = len(args) - hbm, len(outs) - out_hbm
    args = list(args[:smem]) + [local(arg) for arg in args[smem:inside]] + [
        pltpu.with_memory_space_constraint(arg, pltpu.HBM) for arg in args[inside:]
    ]
    room = sum(size_of(item) for item in scratch) + (8 << 20)
    scratch = list(scratch) + ([] if sems is None else [pltpu.SemaphoreType.DMA(sems)])
    results = pl.pallas_call(
        kernel,
        out_shape=[pltpu.VMEM(out.shape, out.dtype) for out in outs[:kept]] + outs[kept:],
        in_specs=[pl.BlockSpec(memory_space=pltpu.SMEM)] * smem
        + vmem(inside - smem)
        + [pl.BlockSpec(memory_space=pltpu.HBM)] * hbm,
        out_specs=vmem(kept) + [pl.BlockSpec(memory_space=pltpu.HBM)] * out_hbm,
        scratch_shapes=scratch,
        compiler_params=pltpu.CompilerParams(vmem_limit_bytes=room),
    )(*args)
    return results if many else results[0]


def swap(block, step, size):
    return lax.ppermute(block, "seq", [(i, i ^ step) for i in range(size)])


def order_of(size):
    return list(range(0, size, 2)) + list(range(1, size, 2))


def by_permutes(size):
    return size in (2, 4, 8)


def gather_near(block, size):
    if not by_permutes(size):
        return lax.all_gather(block, "seq", axis=0)
    return [block] + [swap(block, step, size) for step in range(2, size, 2)]


def gather_far(near, size):
    if not by_permutes(size):
        me = lax.axis_index("seq")
        return [lax.dynamic_index_in_dim(near, me ^ step, 0, False) for step in order_of(size)]
    return near + [swap(piece, 1, size) for piece in near]


def on_device(
    size,
    forward_input,
    stored_input,
    output_cotangent,
    norm_gain,
    query_weight,
    key_weight,
    value_weight,
    output_weight,
    frame_index,
    valid_counts,
):
    xf_hbm, xb_hbm, cot_hbm = forward_input[0], stored_input[0], output_cotangent[0]
    wq_hbm, wk_hbm, wv_hbm, wo_hbm = query_weight[0], key_weight[0], value_weight[0], output_weight[0]
    rows, width = xf_hbm.shape
    total = rows * size
    sections = lax.axis_size("section")
    order = order_of(size)
    half = size // 2
    kv_shape = shape((rows, 2 * KV_COLS), BF16)
    spread = shape((HEADS * rows, KV_COLS), BF16)
    wide = 2 * rows
    gain = local(norm_gain)
    frames = frame_index.reshape(size, rows)
    me = lax.axis_index("seq").astype(jnp.int32).reshape(1)

    kv, xf, xb, wk, wv = call(
        project_kv,
        (shape((rows, 4 * KV_COLS), BF16),) + tuple(shape(item.shape, BF16) for item in (xf_hbm, xb_hbm, wk_hbm, wv_hbm)),
        (gain, xf_hbm, xb_hbm, wk_hbm, wv_hbm),
        sems=(4,),
        hbm=4,
    )
    near = gather_near(kv, size)
    qf, qb, dout, bias, cot, wq, wo = call(
        partial(prepare, order),
        (spread, spread, spread, shape((total, rows), F32))
        + tuple(shape(item.shape, BF16) for item in (cot_hbm, wq_hbm, wo_hbm)),
        (me, valid_counts, xf, xb, gain, frames, cot_hbm, wq_hbm, wo_hbm),
        sems=(3,),
        smem=2,
        hbm=3,
    )
    pieces = gather_far(near, size)
    layer_out = call(
        partial(attend_forward, size),
        shape((rows, width), BF16),
        (*pieces, qf, bias, xf, wo),
        scratch=(
            pltpu.VMEM((total, 2 * KV_COLS), BF16),
            pltpu.VMEM((total, wide), F32),
            pltpu.VMEM((total, wide), BF16),
            pltpu.VMEM((HEADS * HEAD_DIM, rows), F32),
        ),
    )
    shifted = lax.ppermute(layer_out, "section", [((i - 1) % sections, i) for i in range(sections)])
    *grads, dq = call(
        partial(attend_backward, size),
        (kv_shape,) * half + (shape((half, rows, 2 * KV_COLS), BF16), shape((rows, HEADS * HEAD_DIM), BF16)),
        (*pieces, qb, dout, bias),
        scratch=(
            pltpu.VMEM((total, 2 * KV_COLS), BF16),
            pltpu.VMEM((total, wide), F32),
            pltpu.VMEM((total, wide), F32),
            pltpu.VMEM((total, HEADS * rows), BF16),
            pltpu.VMEM((total, HEADS * rows), BF16),
            pltpu.VMEM((HEADS, rows), F32),
            pltpu.VMEM((HEADS * HEAD_DIM, rows), F32),
            pltpu.VMEM((HEADS * rows, KV_COLS), BF16),
            pltpu.VMEM((HEADS * rows, KV_COLS), BF16),
        ),
    )
    even, odd = grads[:half], grads[half]
    if by_permutes(size):
        other = swap(odd, 1, size)
        sums = call(partial(add_pieces, half), (kv_shape,) * half, (*even, other))
        received = [sums[0]] + [swap(sums[i], 2 * i, size) for i in range(1, half)]
    else:
        both = jnp.stack(list(even) + [odd[i] for i in range(half)]).astype(F32)
        places = jnp.argsort(jnp.array(order, jnp.int32) ^ lax.axis_index("seq"))
        summed = lax.psum_scatter(both[places], "seq", scatter_dimension=0, tiled=True)
        received = [summed[0].astype(BF16)]
    base, forward_next = call(
        query_back, (shape((rows, width), F32), shape((rows, width), BF16)), (dq, wq, shifted), sems=(), out_hbm=1
    )
    input_grad = call(
        partial(input_back, len(received)), shape((rows, width), BF16), (*received, base, xb, cot, gain, wk, wv)
    )
    backward_next = lax.ppermute(input_grad, "section", [((i + 1) % sections, i) for i in range(sections)])
    return (forward_next[None], backward_next[None])


def placed(size, *arrays):
    return on_device(size, *arrays)


def solution(mesh):
    size = mesh.shape["seq"]
    return jax.shard_map(
        partial(placed, size),
        mesh=mesh,
        in_specs=(
            P("section", "seq", None),
            P("section", "seq", None),
            P("section", "seq", None),
            P("section", None),
            P("section", None, None),
            P("section", None, None),
            P("section", None, None),
            P("section", None, None),
            P(),
            P(),
        ),
        out_specs=(P("section", "seq", None), P("section", "seq", None)),
        check_vma=False,
    )
```

```python
from functools import partial
import math

import jax
import jax.numpy as jnp
from jax import lax
from jax.experimental import pallas as pl
from jax.experimental.pallas import tpu as pltpu
from jax.sharding import PartitionSpec as P


HEADS = 8
KV_HEADS = 2
HEAD_DIM = 64
GROUP = HEADS // KV_HEADS
KV_COLS = KV_HEADS * HEAD_DIM
PAIRS = HEADS // 2

NORM_EPSILON = 1e-05
MASKED_SCORE = -1e30

F32 = jnp.float32
BF16 = jnp.bfloat16

NN = (((1,), (0,)), ((), ()))
NT = (((1,), (1,)), ((), ()))


def dot(a, b, dims=NN):
    return lax.dot_general(a, b, dims, preferred_element_type=F32)


def vmem(count):
    return [pl.BlockSpec(memory_space=pltpu.VMEM)] * count


def shape(dims, dtype):
    return jax.ShapeDtypeStruct(dims, dtype)


def rms(inputs, gain):
    widened = inputs.astype(F32)
    inverse = lax.rsqrt(jnp.mean(widened * widened, axis=-1, keepdims=True) + NORM_EPSILON)
    return (widened * inverse * gain).astype(BF16), inverse, widened


def project_kv(gain_hbm, xf_hbm, xb_hbm, wk_hbm, wv_hbm, kv_ref, gain_ref, xf_ref, xb_ref, wkv_ref, sems):
    copies = [
        pltpu.make_async_copy(source, target, sems.at[place])
        for place, (source, target) in enumerate(
            (
                (xf_hbm, xf_ref),
                (gain_hbm, gain_ref),
                (xb_hbm, xb_ref),
                (wk_hbm, wkv_ref.at[:, :KV_COLS]),
                (wv_hbm, wkv_ref.at[:, KV_COLS:]),
            )
        )
    ]
    for copy in copies:
        copy.start()
    rows = xf_ref.shape[0]
    copies[0].wait()
    copies[1].wait()
    gain = gain_ref[...]
    normed_f, _, _ = rms(xf_ref[...], gain)
    copies[2].wait()
    normed_b, _, _ = rms(xb_ref[...], gain)
    normed = jnp.concatenate([normed_f, normed_b], axis=0)
    copies[3].wait()
    copies[4].wait()
    both = dot(normed, wkv_ref[...]).astype(BF16)
    kv_ref[:, : 2 * KV_COLS] = both[:rows]
    kv_ref[:, 2 * KV_COLS :] = both[rows:]


def spread_heads(flat, out_ref, scale):
    rows = flat.shape[0]
    flat = flat.astype(BF16).astype(F32) * scale
    lane = lax.broadcasted_iota(jnp.int32, (rows, KV_COLS), 1)
    for head in range(HEADS):
        tile = head // 2
        block = flat[:, tile * KV_COLS : (tile + 1) * KV_COLS]
        group = head // GROUP
        if head % 2 != group:
            block = pltpu.roll(block, HEAD_DIM, 1)
        block = jnp.where((lane // HEAD_DIM) == group, block, 0.0)
        out_ref[head * rows : (head + 1) * rows, :] = block.astype(BF16)


def prepare(
    order,
    me_ref,
    xf_ref,
    xb_ref,
    gain_ref,
    frames_hbm,
    counts_hbm,
    cot_hbm,
    wq_hbm,
    wo_hbm,
    qf_ref,
    qb_ref,
    dout_ref,
    bias_ref,
    cot_ref,
    wq_ref,
    wo_ref,
    frames_ref,
    counts_ref,
    sems,
):
    copies = [
        pltpu.make_async_copy(source, target, sems.at[place])
        for place, (source, target) in enumerate(
            (
                (wq_hbm, wq_ref),
                (frames_hbm, frames_ref),
                (counts_hbm, counts_ref),
                (cot_hbm, cot_ref),
                (wo_hbm, wo_ref),
            )
        )
    ]
    for copy in copies:
        copy.start()
    gain = gain_ref[...]
    rows = xf_ref.shape[0]
    normed_f, _, _ = rms(xf_ref[...], gain)
    normed_b, _, _ = rms(xb_ref[...], gain)
    copies[1].wait()
    copies[2].wait()
    me = me_ref[0]
    row = lax.broadcasted_iota(jnp.int32, (rows, rows), 0)
    query_frames = jnp.broadcast_to(frames_ref[pl.ds(me, 1), :], (rows, rows))
    for place, step in enumerate(order):
        source = jnp.bitwise_xor(me, step)
        own = jnp.broadcast_to(frames_ref[pl.ds(source, 1), :], (rows, rows))
        key_frames = jnp.transpose(own.astype(F32)).astype(jnp.int32)
        visible = (key_frames <= query_frames) & (row < counts_ref[source])
        bias_ref[place * rows : (place + 1) * rows, :] = jnp.where(visible, 0.0, MASKED_SCORE)
    scale = 1.0 / math.sqrt(HEAD_DIM)
    copies[0].wait()
    queries = dot(jnp.concatenate([normed_f, normed_b], axis=0), wq_ref[...])
    spread_heads(queries[:rows], qf_ref, scale)
    spread_heads(queries[rows:], qb_ref, scale)
    copies[3].wait()
    copies[4].wait()
    spread_heads(dot(cot_ref[...], wo_ref[...], NT), dout_ref, 1.0)


def score_block(keys, q_rows, bias_ref, s_ref, slot, lines, top):
    block = dot(keys[lines], q_rows, NT)
    bias = bias_ref[lines, :]
    block = block + jnp.concatenate([bias, bias], axis=1)
    s_ref[slot, lines, :] = block
    part = jnp.max(block, axis=0, keepdims=True)
    return part if top is None else jnp.maximum(top, part)


def plus(left, right):
    return right if left is None else left + right


def attend_backward(count, *refs):
    pieces = refs[:count]
    q_ref, dout_ref, bias_ref = refs[count : count + 3]
    half = count // 2
    even_refs = refs[count + 3 : count + 3 + half]
    odd_ref, dq_ref = refs[count + 3 + half : count + 5 + half]
    kv_ref, s_ref, dp_ref, e_ref, acc_ref, dqt_ref = refs[count + 5 + half :]
    rows = pieces[0].shape[0]
    total = rows * count
    chunk = min(4 * rows, total)
    for place, piece in enumerate(pieces):
        kv_ref[place * rows : (place + 1) * rows, :] = piece[:, 2 * KV_COLS :]
    keys = kv_ref[:, :KV_COLS]
    values = kv_ref[:, KV_COLS:]
    keys_t = jnp.transpose(keys)
    scale = 1.0 / math.sqrt(HEAD_DIM)
    wide = 2 * rows
    tops, stats, scaled = {}, {}, {}
    for step in range(-1, PAIRS + 1):
        ahead, now, behind = step + 1, step, step - 1
        top = row_sum = mixed = query_grad = None
        for first in range(0, total, chunk):
            lines = slice(first, first + chunk)
            if ahead < PAIRS:
                q_rows = q_ref[ahead * wide : (ahead + 1) * wide, :]
                top = score_block(keys, q_rows, bias_ref, s_ref, ahead % 2, lines, top)
            if 0 <= now < PAIRS:
                slot = now % 2
                weights = jnp.exp(s_ref[slot, lines, :] - tops[now])
                prob_grad = dot(values[lines], dout_ref[now * wide : (now + 1) * wide, :], NT)
                row_sum = plus(row_sum, jnp.sum(weights, axis=0, keepdims=True))
                mixed = plus(mixed, jnp.sum(weights * prob_grad, axis=0, keepdims=True))
                dp_ref[slot, lines, :] = prob_grad
                e_ref[slot, lines, :] = weights.astype(BF16)
            if behind >= 0:
                slot = behind % 2
                weights = e_ref[slot, lines, :]
                score_grad = weights * (dp_ref[slot, lines, :] - stats[behind][1]).astype(BF16)
                group = (2 * behind) // GROUP
                own = slice(group * HEAD_DIM, (group + 1) * HEAD_DIM)
                query_grad = plus(query_grad, dot(keys_t[own, lines], score_grad))
                key_grad = dot(score_grad, scaled[behind][0])
                value_grad = dot(weights, scaled[behind][1])
                if behind:
                    key_grad = key_grad + acc_ref[lines, :KV_COLS]
                    value_grad = value_grad + acc_ref[lines, KV_COLS:]
                if behind < PAIRS - 1:
                    acc_ref[lines, :KV_COLS] = key_grad
                    acc_ref[lines, KV_COLS:] = value_grad
                else:
                    for place in range(first // rows, (first + chunk) // rows):
                        target = even_refs[place] if place < half else odd_ref.at[place - half]
                        inner = slice(place * rows - first, (place + 1) * rows - first)
                        target[:, :KV_COLS] = key_grad[inner].astype(BF16)
                        target[:, KV_COLS:] = value_grad[inner].astype(BF16)
        if ahead < PAIRS:
            tops[ahead] = top
        if 0 <= now < PAIRS:
            inverse_sum = 1.0 / row_sum
            stats[now] = (inverse_sum, mixed * inverse_sum)
            cols = slice(now * wide, (now + 1) * wide)
            factor = jnp.transpose(jnp.broadcast_to(inverse_sum, (KV_COLS, wide)))
            scaled[now] = (
                (q_ref[cols, :].astype(F32) * factor).astype(BF16),
                (dout_ref[cols, :].astype(F32) * factor).astype(BF16),
            )
        if behind >= 0:
            part = query_grad * (stats[behind][0] * scale)
            dqt_ref[2 * behind * HEAD_DIM : (2 * behind + 1) * HEAD_DIM, :] = part[:, :rows]
            dqt_ref[(2 * behind + 1) * HEAD_DIM : (2 * behind + 2) * HEAD_DIM, :] = part[:, rows:]
    dq_ref[...] = jnp.transpose(dqt_ref[...]).astype(BF16)


def attend_forward(count, *refs):
    pieces = refs[:count]
    q_ref, bias_ref, x_ref, wo_ref, out_ref = refs[count : count + 5]
    kv_ref, s_ref, at_ref = refs[count + 5 :]
    rows = pieces[0].shape[0]
    total = rows * count
    chunk = min(4 * rows, total)
    for place, piece in enumerate(pieces):
        kv_ref[place * rows : (place + 1) * rows, :] = piece[:, : 2 * KV_COLS]
    keys = kv_ref[:, :KV_COLS]
    values_t = jnp.transpose(kv_ref[:, KV_COLS:])
    ones = jnp.ones((16, total), BF16)
    extended = [
        jnp.concatenate([values_t[group * HEAD_DIM : (group + 1) * HEAD_DIM], ones], axis=0)
        for group in range(KV_HEADS)
    ]
    wide = 2 * rows
    tops = {}
    for now in range(-1, PAIRS):
        ahead = now + 1
        top = mixed = None
        for first in range(0, total, chunk):
            lines = slice(first, first + chunk)
            if ahead < PAIRS:
                q_rows = q_ref[ahead * wide : (ahead + 1) * wide, :]
                top = score_block(keys, q_rows, bias_ref, s_ref, ahead % 2, lines, top)
            if now >= 0:
                weights = jnp.exp(s_ref[now % 2, lines, :] - tops[now])
                mixed = plus(mixed, dot(extended[(2 * now) // GROUP][:, lines], weights.astype(BF16)))
        if ahead < PAIRS:
            tops[ahead] = top
        if now >= 0:
            part = mixed[:HEAD_DIM] * (1.0 / mixed[HEAD_DIM : HEAD_DIM + 1])
            at_ref[2 * now * HEAD_DIM : (2 * now + 1) * HEAD_DIM, :] = part[:, :rows]
            at_ref[(2 * now + 1) * HEAD_DIM : (2 * now + 2) * HEAD_DIM, :] = part[:, rows:]
    attended = jnp.transpose(at_ref[...]).astype(BF16)
    out_ref[...] = (x_ref[...].astype(F32) + dot(attended, wo_ref[...])).astype(BF16)


def query_back(dq_ref, wq_ref, next_ref, out_ref, next_hbm, sem):
    copy = pltpu.make_async_copy(next_ref, next_hbm, sem)
    copy.start()
    out_ref[...] = dot(dq_ref[...], wq_ref[...], NT)
    copy.wait()


def add_pieces(count, *refs):
    for place in range(count):
        left = refs[place][...].astype(F32)
        refs[count + 1 + place][...] = (left + refs[count][place].astype(F32)).astype(BF16)


def input_back(count, *refs):
    pieces = refs[:count]
    base_ref, x_ref, cot_ref, gain_ref, wkv_ref, out_ref = refs[count:]
    grads = pieces[0][...].astype(F32)
    for piece in pieces[1:]:
        grads = grads + piece[...].astype(F32)
    grads = grads.astype(BF16)
    gain = gain_ref[...]
    normed_grad = base_ref[...] + dot(grads, wkv_ref[...], NT)
    _, inverse, widened = rms(x_ref[...], gain)
    scaled = normed_grad * gain
    mean = jnp.mean(widened * scaled, axis=-1, keepdims=True)
    grad = cot_ref[...].astype(F32) + inverse * scaled - widened * (inverse * inverse * inverse * mean)
    out_ref[...] = grad.astype(BF16)


def local(array):
    return pltpu.with_memory_space_constraint(array, pltpu.VMEM)


def size_of(item):
    return math.prod(item.shape) * jnp.dtype(item.dtype).itemsize


def call(kernel, outs, args, scratch=(), sems=None, smem=0, hbm=0, out_hbm=0):
    many = isinstance(outs, (list, tuple))
    outs = list(outs) if many else [outs]
    inside, kept = len(args) - hbm, len(outs) - out_hbm
    args = list(args[:smem]) + [local(arg) for arg in args[smem:inside]] + [
        pltpu.with_memory_space_constraint(arg, pltpu.HBM) for arg in args[inside:]
    ]
    room = sum(size_of(item) for item in scratch) + (8 << 20)
    scratch = list(scratch) + ([] if sems is None else [pltpu.SemaphoreType.DMA(sems)])
    results = pl.pallas_call(
        kernel,
        out_shape=[pltpu.VMEM(out.shape, out.dtype) for out in outs[:kept]] + outs[kept:],
        in_specs=[pl.BlockSpec(memory_space=pltpu.SMEM)] * smem
        + vmem(inside - smem)
        + [pl.BlockSpec(memory_space=pltpu.HBM)] * hbm,
        out_specs=vmem(kept) + [pl.BlockSpec(memory_space=pltpu.HBM)] * out_hbm,
        scratch_shapes=scratch,
        compiler_params=pltpu.CompilerParams(vmem_limit_bytes=room),
    )(*args)
    return results if many else results[0]


def swap(block, step, size):
    return lax.ppermute(block, "seq", [(i, i ^ step) for i in range(size)])


def order_of(size):
    return list(range(0, size, 2)) + list(range(1, size, 2))


def by_permutes(size):
    return size in (2, 4, 8)


def gather_near(block, size):
    if not by_permutes(size):
        return lax.all_gather(block, "seq", axis=0)
    return [block] + [swap(block, step, size) for step in range(2, size, 2)]


def gather_far(near, size):
    if not by_permutes(size):
        me = lax.axis_index("seq")
        return [lax.dynamic_index_in_dim(near, me ^ step, 0, False) for step in order_of(size)]
    return near + [swap(piece, 1, size) for piece in near]


def on_device(
    size,
    forward_input,
    stored_input,
    output_cotangent,
    norm_gain,
    query_weight,
    key_weight,
    value_weight,
    output_weight,
    frame_index,
    valid_counts,
):
    xf_hbm, xb_hbm, cot_hbm = forward_input[0], stored_input[0], output_cotangent[0]
    wq_hbm, wk_hbm, wv_hbm, wo_hbm = query_weight[0], key_weight[0], value_weight[0], output_weight[0]
    rows, width = xf_hbm.shape
    total = rows * size
    sections = lax.axis_size("section")
    order = order_of(size)
    half = size // 2
    kv_shape = shape((rows, 2 * KV_COLS), BF16)
    spread = shape((HEADS * rows, KV_COLS), BF16)
    wide = 2 * rows
    frames = frame_index.reshape(size, rows)
    me = lax.axis_index("seq").astype(jnp.int32).reshape(1)

    kv, gain, xf, xb, wkv = call(
        project_kv,
        (
            shape((rows, 4 * KV_COLS), BF16),
            shape(norm_gain.shape, F32),
            shape(xf_hbm.shape, BF16),
            shape(xb_hbm.shape, BF16),
            shape((width, 2 * KV_COLS), BF16),
        ),
        (norm_gain, xf_hbm, xb_hbm, wk_hbm, wv_hbm),
        sems=(5,),
        hbm=5,
    )
    near = gather_near(kv, size)
    qf, qb, dout, bias, cot, wq, wo = call(
        partial(prepare, order),
        (spread, spread, spread, shape((total, rows), F32))
        + tuple(shape(item.shape, BF16) for item in (cot_hbm, wq_hbm, wo_hbm)),
        (me, xf, xb, gain, frames, valid_counts, cot_hbm, wq_hbm, wo_hbm),
        scratch=(pltpu.VMEM(frames.shape, jnp.int32), pltpu.SMEM(valid_counts.shape, jnp.int32)),
        sems=(5,),
        smem=1,
        hbm=5,
    )
    pieces = gather_far(near, size)
    layer_out = call(
        partial(attend_forward, size),
        shape((rows, width), BF16),
        (*pieces, qf, bias, xf, wo),
        scratch=(
            pltpu.VMEM((total, 2 * KV_COLS), BF16),
            pltpu.VMEM((2, total, wide), F32),
            pltpu.VMEM((HEADS * HEAD_DIM, rows), F32),
        ),
    )
    shifted = lax.ppermute(layer_out, "section", [((i - 1) % sections, i) for i in range(sections)])
    *grads, dq = call(
        partial(attend_backward, size),
        (kv_shape,) * half + (shape((half, rows, 2 * KV_COLS), BF16), shape((rows, HEADS * HEAD_DIM), BF16)),
        (*pieces, qb, dout, bias),
        scratch=(
            pltpu.VMEM((total, 2 * KV_COLS), BF16),
            pltpu.VMEM((2, total, wide), F32),
            pltpu.VMEM((2, total, wide), F32),
            pltpu.VMEM((2, total, wide), BF16),
            pltpu.VMEM((total, 2 * KV_COLS), F32),
            pltpu.VMEM((HEADS * HEAD_DIM, rows), F32),
        ),
    )
    even, odd = grads[:half], grads[half]
    if by_permutes(size):
        other = swap(odd, 1, size)
        sums = call(partial(add_pieces, half), (kv_shape,) * half, (*even, other))
        received = [sums[0]] + [swap(sums[i], 2 * i, size) for i in range(1, half)]
    else:
        both = jnp.stack(list(even) + [odd[i] for i in range(half)]).astype(F32)
        places = jnp.argsort(jnp.array(order, jnp.int32) ^ lax.axis_index("seq"))
        summed = lax.psum_scatter(both[places], "seq", scatter_dimension=0, tiled=True)
        received = [summed[0].astype(BF16)]
    base, forward_next = call(
        query_back, (shape((rows, width), F32), shape((rows, width), BF16)), (dq, wq, shifted), sems=(), out_hbm=1
    )
    input_grad = call(
        partial(input_back, len(received)), shape((rows, width), BF16), (*received, base, xb, cot, gain, wkv)
    )
    backward_next = lax.ppermute(input_grad, "section", [((i + 1) % sections, i) for i in range(sections)])
    return (forward_next[None], backward_next[None])


def placed(size, *arrays):
    return on_device(size, *arrays)


def solution(mesh):
    size = mesh.shape["seq"]
    return jax.shard_map(
        partial(placed, size),
        mesh=mesh,
        in_specs=(
            P("section", "seq", None),
            P("section", "seq", None),
            P("section", "seq", None),
            P("section", None),
            P("section", None, None),
            P("section", None, None),
            P("section", None, None),
            P("section", None, None),
            P(),
            P(),
        ),
        out_specs=(P("section", "seq", None), P("section", "seq", None)),
        check_vma=False,
    )
```

```python
from functools import partial
import math

import jax
import jax.numpy as jnp
from jax import lax
from jax.experimental import pallas as pl
from jax.experimental.pallas import tpu as pltpu
from jax.sharding import PartitionSpec as P


HEADS = 8
KV_HEADS = 2
HEAD_DIM = 64
GROUP = HEADS // KV_HEADS
KV_COLS = KV_HEADS * HEAD_DIM
PAIRS = HEADS // 2

NORM_EPSILON = 1e-05
MASKED_SCORE = -1e30

F32 = jnp.float32
BF16 = jnp.bfloat16

NN = (((1,), (0,)), ((), ()))
NT = (((1,), (1,)), ((), ()))


def dot(a, b, dims=NN):
    return lax.dot_general(a, b, dims, preferred_element_type=F32)


def vmem(count):
    return [pl.BlockSpec(memory_space=pltpu.VMEM)] * count


def shape(dims, dtype):
    return jax.ShapeDtypeStruct(dims, dtype)


def rms(inputs, gain):
    widened = inputs.astype(F32)
    inverse = lax.rsqrt(jnp.mean(widened * widened, axis=-1, keepdims=True) + NORM_EPSILON)
    return (widened * inverse * gain).astype(BF16), inverse, widened


def project_kv(gain_hbm, xf_hbm, xb_hbm, wk_hbm, wv_hbm, kv_ref, gain_ref, xf_ref, xb_ref, wkv_ref, sems):
    copies = [
        pltpu.make_async_copy(source, target, sems.at[place])
        for place, (source, target) in enumerate(
            (
                (xf_hbm, xf_ref),
                (gain_hbm, gain_ref),
                (xb_hbm, xb_ref),
                (wk_hbm, wkv_ref.at[:, :KV_COLS]),
                (wv_hbm, wkv_ref.at[:, KV_COLS:]),
            )
        )
    ]
    for copy in copies:
        copy.start()
    rows = xf_ref.shape[0]
    copies[0].wait()
    copies[1].wait()
    gain = gain_ref[...]
    normed_f, _, _ = rms(xf_ref[...], gain)
    copies[2].wait()
    normed_b, _, _ = rms(xb_ref[...], gain)
    normed = jnp.concatenate([normed_f, normed_b], axis=0)
    copies[3].wait()
    copies[4].wait()
    both = dot(normed, wkv_ref[...]).astype(BF16)
    kv_ref[:, : 2 * KV_COLS] = both[:rows]
    kv_ref[:, 2 * KV_COLS :] = both[rows:]


def spread_heads(flat, out_ref, scale):
    rows = flat.shape[0]
    flat = flat.astype(BF16).astype(F32) * scale
    lane = lax.broadcasted_iota(jnp.int32, (rows, KV_COLS), 1)
    for head in range(HEADS):
        tile = head // 2
        block = flat[:, tile * KV_COLS : (tile + 1) * KV_COLS]
        group = head // GROUP
        if head % 2 != group:
            block = pltpu.roll(block, HEAD_DIM, 1)
        block = jnp.where((lane // HEAD_DIM) == group, block, 0.0)
        out_ref[head * rows : (head + 1) * rows, :] = block.astype(BF16)


def prepare(
    order,
    me_ref,
    xf_ref,
    xb_ref,
    gain_ref,
    frames_hbm,
    counts_hbm,
    cot_hbm,
    wq_hbm,
    wo_hbm,
    qf_ref,
    qb_ref,
    dout_ref,
    bias_ref,
    cot_ref,
    wq_ref,
    wo_ref,
    frames_ref,
    counts_ref,
    sems,
):
    copies = [
        pltpu.make_async_copy(source, target, sems.at[place])
        for place, (source, target) in enumerate(
            (
                (wq_hbm, wq_ref),
                (frames_hbm, frames_ref),
                (counts_hbm, counts_ref),
                (cot_hbm, cot_ref),
                (wo_hbm, wo_ref),
            )
        )
    ]
    for copy in copies:
        copy.start()
    gain = gain_ref[...]
    rows = xf_ref.shape[0]
    normed_f, _, _ = rms(xf_ref[...], gain)
    normed_b, _, _ = rms(xb_ref[...], gain)
    copies[1].wait()
    copies[2].wait()
    me = me_ref[0]
    row = lax.broadcasted_iota(jnp.int32, (rows, rows), 0)
    query_frames = jnp.broadcast_to(frames_ref[pl.ds(me, 1), :], (rows, rows))
    for place, step in enumerate(order):
        source = jnp.bitwise_xor(me, step)
        own = jnp.broadcast_to(frames_ref[pl.ds(source, 1), :], (rows, rows))
        key_frames = jnp.transpose(own.astype(F32)).astype(jnp.int32)
        visible = (key_frames <= query_frames) & (row < counts_ref[source])
        bias_ref[place * rows : (place + 1) * rows, :] = jnp.where(visible, 0.0, MASKED_SCORE)
    scale = 1.0 / math.sqrt(HEAD_DIM)
    copies[0].wait()
    queries = dot(jnp.concatenate([normed_f, normed_b], axis=0), wq_ref[...])
    spread_heads(queries[:rows], qf_ref, scale)
    spread_heads(queries[rows:], qb_ref, scale)
    copies[3].wait()
    copies[4].wait()
    spread_heads(dot(cot_ref[...], wo_ref[...], NT), dout_ref, 1.0)


def plus(left, right):
    return right if left is None else left + right


def twice(bias):
    return jnp.concatenate([bias, bias], axis=1)


def score_block(keys, q_rows, bias):
    return dot(keys, q_rows, NT) + twice(bias)


def with_ones(values):
    values_t = jnp.transpose(values)
    ones = jnp.ones((16, values.shape[0]), BF16)
    return [
        jnp.concatenate([values_t[group * HEAD_DIM : (group + 1) * HEAD_DIM], ones], axis=0)
        for group in range(KV_HEADS)
    ]


def late_chunks(count, rows):
    half = count // 2
    pieces = 3 if (half - 1) % 3 == 0 else 1
    starts = list(range(1, half, pieces)) + list(range(half, count - 1, pieces))
    return [slice(start * rows, (start + pieces) * rows) for start in starts]


def attend_early(far_ref, own_ref, qf_ref, qb_ref, dout_ref, bias_ref, top_ref, mix_ref, stat_ref, e_ref, dp_ref):
    rows = own_ref.shape[0]
    pieces = jnp.concatenate([far_ref[...], own_ref[...]], axis=0)
    bias = jnp.concatenate([bias_ref[:rows, :], bias_ref[-rows:, :]], axis=0)
    extended = with_ones(pieces[:, KV_COLS : 2 * KV_COLS])
    wide = 2 * rows
    for pair in range(PAIRS):
        cols = slice(pair * wide, (pair + 1) * wide)
        block = score_block(pieces[:, :KV_COLS], qf_ref[cols, :], bias)
        top = jnp.max(block, axis=0, keepdims=True)
        top_ref[pair : pair + 1, :] = top
        weights = jnp.exp(block - top).astype(BF16)
        mix_ref[pair] = dot(extended[(2 * pair) // GROUP], weights)
        block = score_block(pieces[:, 2 * KV_COLS : 3 * KV_COLS], qb_ref[cols, :], bias)
        top = jnp.max(block, axis=0, keepdims=True)
        weights = jnp.exp(block - top)
        prob_grad = dot(pieces[:, 3 * KV_COLS :], dout_ref[cols, :], NT)
        stat_ref[0:1, cols] = top
        stat_ref[1:2, cols] = jnp.sum(weights, axis=0, keepdims=True)
        stat_ref[2:3, cols] = jnp.sum(weights * prob_grad, axis=0, keepdims=True)
        e_ref[:, cols] = weights.astype(BF16)
        dp_ref[:, cols] = prob_grad


def attend_backward(count, *refs):
    pieces = refs[: count - 2]
    q_ref, dout_ref, bias_ref, far_ref, own_ref, stat_ref, e1_ref, dp1_ref = refs[count - 2 : count + 6]
    odd_ref, u_ref, e_ref, qs_ref, ds_ref, keys_ref, rs_ref = refs[count + 6 : count + 13]
    values_ref, s_ref, dp_ref, acc_ref = refs[count + 13 :]
    rows = own_ref.shape[0]
    total = rows * count
    half = count // 2
    odd = slice(0, half * rows)
    for place, piece in enumerate((far_ref, *pieces, own_ref)):
        lines = slice(place * rows, (place + 1) * rows)
        keys_ref[lines, :] = piece[:, 2 * KV_COLS : 3 * KV_COLS]
        values_ref[lines, :] = piece[:, 3 * KV_COLS :]
    scale = 1.0 / math.sqrt(HEAD_DIM)
    wide = 2 * rows
    chunks = late_chunks(count, rows)
    tops, stats, scaled = {}, {}, {}
    for step in range(-1, PAIRS + 1):
        ahead, now, behind = step + 1, step, step - 1
        top = row_sum = mixed = None
        if behind >= 0:
            cols = slice(behind * wide, (behind + 1) * wide)
            delta, factor = stats[behind]
            weights = e1_ref[:, cols].astype(F32) * factor
            score_grad = (weights * (dp1_ref[:, cols] - delta)).astype(BF16)
            weights = weights.astype(BF16)
            for lines, part in ((slice(0, rows), slice(0, rows)), (slice(total - rows, total), slice(rows, wide))):
                e_ref[lines, cols] = weights[part]
                u_ref[lines, cols] = score_grad[part]
        for lines in chunks:
            if 0 <= now < PAIRS:
                cols = slice(now * wide, (now + 1) * wide)
                weights = jnp.exp(s_ref[now % 2, lines, :] - tops[now])
                prob_grad = dot(values_ref[lines, :], dout_ref[cols, :], NT)
                row_sum = plus(row_sum, jnp.sum(weights, axis=0, keepdims=True))
                mixed = plus(mixed, jnp.sum(weights * prob_grad, axis=0, keepdims=True))
                dp_ref[now % 2, lines, :] = prob_grad
                e_ref[lines, cols] = weights.astype(BF16)
            if ahead < PAIRS:
                q_rows = q_ref[ahead * wide : (ahead + 1) * wide, :]
                block = score_block(keys_ref[lines, :], q_rows, bias_ref[lines, :])
                s_ref[ahead % 2, lines, :] = block
                part = jnp.max(block, axis=0, keepdims=True)
                top = part if top is None else jnp.maximum(top, part)
            if behind >= 0:
                cols = slice(behind * wide, (behind + 1) * wide)
                difference = (dp_ref[behind % 2, lines, :] - stats[behind][0]).astype(BF16)
                u_ref[lines, cols] = e_ref[lines, cols] * difference
                if lines.stop == odd.stop:
                    key_grad = dot(u_ref[odd, cols], scaled[behind][0])
                    value_grad = dot(e_ref[odd, cols], scaled[behind][1])
                    if behind:
                        key_grad = key_grad + acc_ref[:, :KV_COLS]
                        value_grad = value_grad + acc_ref[:, KV_COLS:]
                    if behind < PAIRS - 1:
                        acc_ref[:, :KV_COLS] = key_grad
                        acc_ref[:, KV_COLS:] = value_grad
                    else:
                        for place in range(half):
                            inner = slice(place * rows, (place + 1) * rows)
                            odd_ref[place, :, :KV_COLS] = key_grad[inner].astype(BF16)
                            odd_ref[place, :, KV_COLS:] = value_grad[inner].astype(BF16)
        if ahead < PAIRS:
            tops[ahead] = jnp.maximum(top, stat_ref[0:1, ahead * wide : (ahead + 1) * wide])
        if 0 <= now < PAIRS:
            cols = slice(now * wide, (now + 1) * wide)
            factor = jnp.exp(stat_ref[0:1, cols] - tops[now])
            inverse_sum = 1.0 / (row_sum + factor * stat_ref[1:2, cols])
            stats[now] = ((mixed + factor * stat_ref[2:3, cols]) * inverse_sum, factor)
            rs_ref[0:1, cols] = inverse_sum * scale
            column = jnp.transpose(jnp.broadcast_to(inverse_sum, (KV_COLS, wide)))
            scaled[now] = (
                (q_ref[cols, :].astype(F32) * column).astype(BF16),
                (dout_ref[cols, :].astype(F32) * column).astype(BF16),
            )
            qs_ref[cols, :], ds_ref[cols, :] = scaled[now]


def finish_backward(u_ref, e_ref, qs_ref, ds_ref, keys_ref, rs_ref, *refs):
    even_refs, dq_ref, dqt_ref = refs[:-2], refs[-2], refs[-1]
    rows = even_refs[0].shape[0]
    even = slice(len(even_refs) * rows, 2 * len(even_refs) * rows)
    wide = 2 * rows
    key_grad = dot(u_ref[even, :], qs_ref[...]).astype(BF16)
    value_grad = dot(e_ref[even, :], ds_ref[...]).astype(BF16)
    for place, target in enumerate(even_refs):
        target[:, :KV_COLS] = key_grad[place * rows : (place + 1) * rows]
        target[:, KV_COLS:] = value_grad[place * rows : (place + 1) * rows]
    keys_t = jnp.transpose(keys_ref[...])
    for pair in range(PAIRS):
        group = (2 * pair) // GROUP
        cols = slice(pair * wide, (pair + 1) * wide)
        part = dot(keys_t[group * HEAD_DIM : (group + 1) * HEAD_DIM], u_ref[:, cols]) * rs_ref[0:1, cols]
        dqt_ref[2 * pair * HEAD_DIM : (2 * pair + 1) * HEAD_DIM, :] = part[:, :rows]
        dqt_ref[(2 * pair + 1) * HEAD_DIM : (2 * pair + 2) * HEAD_DIM, :] = part[:, rows:]
    dq_ref[...] = jnp.transpose(dqt_ref[...]).astype(BF16)


def attend_forward(count, *refs):
    pieces = refs[: count - 2]
    q_ref, bias_ref, x_ref, wo_ref, top_ref, mix_ref, out_ref = refs[count - 2 : count + 5]
    kv_ref, s_ref, at_ref = refs[count + 5 :]
    rows = pieces[0].shape[0]
    for place, piece in enumerate(pieces):
        kv_ref[(place + 1) * rows : (place + 2) * rows, :] = piece[:, : 2 * KV_COLS]
    chunks = late_chunks(count, rows)
    extended = [with_ones(kv_ref[lines, KV_COLS:]) for lines in chunks]
    wide = 2 * rows
    tops = {}
    for now in range(-1, PAIRS):
        ahead = now + 1
        top = mixed = None
        for place, lines in enumerate(chunks):
            if ahead < PAIRS:
                q_rows = q_ref[ahead * wide : (ahead + 1) * wide, :]
                block = score_block(kv_ref[lines, :KV_COLS], q_rows, bias_ref[lines, :])
                s_ref[ahead % 2, lines, :] = block
                part = jnp.max(block, axis=0, keepdims=True)
                top = part if top is None else jnp.maximum(top, part)
            if now >= 0:
                weights = jnp.exp(s_ref[now % 2, lines, :] - tops[now]).astype(BF16)
                mixed = plus(mixed, dot(extended[place][(2 * now) // GROUP], weights))
        if ahead < PAIRS:
            tops[ahead] = jnp.maximum(top, top_ref[ahead : ahead + 1, :])
        if now >= 0:
            mixed = mixed + mix_ref[now] * jnp.exp(top_ref[now : now + 1, :] - tops[now])
            part = mixed[:HEAD_DIM] * (1.0 / mixed[HEAD_DIM : HEAD_DIM + 1])
            at_ref[2 * now * HEAD_DIM : (2 * now + 1) * HEAD_DIM, :] = part[:, :rows]
            at_ref[(2 * now + 1) * HEAD_DIM : (2 * now + 2) * HEAD_DIM, :] = part[:, rows:]
    attended = jnp.transpose(at_ref[...]).astype(BF16)
    out_ref[...] = (x_ref[...].astype(F32) + dot(attended, wo_ref[...])).astype(BF16)


def query_back(dq_ref, wq_ref, next_ref, out_ref, next_hbm, sem):
    copy = pltpu.make_async_copy(next_ref, next_hbm, sem)
    copy.start()
    out_ref[...] = dot(dq_ref[...], wq_ref[...], NT)
    copy.wait()


def add_pieces(count, *refs):
    for place in range(count):
        left = refs[place][...].astype(F32)
        refs[count + 1 + place][...] = (left + refs[count][(place + 1) % count].astype(F32)).astype(BF16)


def input_back(count, *refs):
    pieces = refs[:count]
    base_ref, x_ref, cot_ref, gain_ref, wkv_ref, out_ref = refs[count:]
    grads = pieces[0][...].astype(F32)
    for piece in pieces[1:]:
        grads = grads + piece[...].astype(F32)
    grads = grads.astype(BF16)
    gain = gain_ref[...]
    normed_grad = base_ref[...] + dot(grads, wkv_ref[...], NT)
    _, inverse, widened = rms(x_ref[...], gain)
    scaled = normed_grad * gain
    mean = jnp.mean(widened * scaled, axis=-1, keepdims=True)
    grad = cot_ref[...].astype(F32) + inverse * scaled - widened * (inverse * inverse * inverse * mean)
    out_ref[...] = grad.astype(BF16)


def local(array):
    return pltpu.with_memory_space_constraint(array, pltpu.VMEM)


def size_of(item):
    return math.prod(item.shape) * jnp.dtype(item.dtype).itemsize


def call(kernel, outs, args, scratch=(), sems=None, smem=0, hbm=0, out_hbm=0):
    many = isinstance(outs, (list, tuple))
    outs = list(outs) if many else [outs]
    inside, kept = len(args) - hbm, len(outs) - out_hbm
    args = list(args[:smem]) + [local(arg) for arg in args[smem:inside]] + [
        pltpu.with_memory_space_constraint(arg, pltpu.HBM) for arg in args[inside:]
    ]
    room = sum(size_of(item) for item in scratch) + (8 << 20)
    scratch = list(scratch) + ([] if sems is None else [pltpu.SemaphoreType.DMA(sems)])
    results = pl.pallas_call(
        kernel,
        out_shape=[pltpu.VMEM(out.shape, out.dtype) for out in outs[:kept]] + outs[kept:],
        in_specs=[pl.BlockSpec(memory_space=pltpu.SMEM)] * smem
        + vmem(inside - smem)
        + [pl.BlockSpec(memory_space=pltpu.HBM)] * hbm,
        out_specs=vmem(kept) + [pl.BlockSpec(memory_space=pltpu.HBM)] * out_hbm,
        scratch_shapes=scratch,
        compiler_params=pltpu.CompilerParams(vmem_limit_bytes=room),
    )(*args)
    return results if many else results[0]


def swap(block, step, size):
    return lax.ppermute(block, "seq", [(i, i ^ step) for i in range(size)])


def order_of(size):
    return list(range(1, size, 2)) + list(range(2, size, 2)) + [0]


def by_permutes(size):
    return size in (4, 8)


def gather_near(block, size):
    if not by_permutes(size):
        return lax.all_gather(block, "seq", axis=0)
    return [block] + [swap(block, step, size) for step in range(2, size, 2)]


def gather_far(near, size):
    if not by_permutes(size):
        me = lax.axis_index("seq")
        return [lax.dynamic_index_in_dim(near, me ^ step, 0, False) for step in order_of(size)]
    far = [swap(piece, 1, size) for piece in near]
    return far + near[1:] + near[:1]


def on_device(
    size,
    forward_input,
    stored_input,
    output_cotangent,
    norm_gain,
    query_weight,
    key_weight,
    value_weight,
    output_weight,
    frame_index,
    valid_counts,
):
    xf_hbm, xb_hbm, cot_hbm = forward_input[0], stored_input[0], output_cotangent[0]
    wq_hbm, wk_hbm, wv_hbm, wo_hbm = query_weight[0], key_weight[0], value_weight[0], output_weight[0]
    rows, width = xf_hbm.shape
    total = rows * size
    sections = lax.axis_size("section")
    order = order_of(size)
    half = size // 2
    kv_shape = shape((rows, 2 * KV_COLS), BF16)
    spread = shape((HEADS * rows, KV_COLS), BF16)
    wide = 2 * rows
    frames = frame_index.reshape(size, rows)
    me = lax.axis_index("seq").astype(jnp.int32).reshape(1)

    kv, gain, xf, xb, wkv = call(
        project_kv,
        (
            shape((rows, 4 * KV_COLS), BF16),
            shape(norm_gain.shape, F32),
            shape(xf_hbm.shape, BF16),
            shape(xb_hbm.shape, BF16),
            shape((width, 2 * KV_COLS), BF16),
        ),
        (norm_gain, xf_hbm, xb_hbm, wk_hbm, wv_hbm),
        sems=(5,),
        hbm=5,
    )
    near = gather_near(kv, size)
    qf, qb, dout, bias, cot, wq, wo = call(
        partial(prepare, order),
        (spread, spread, spread, shape((total, rows), F32))
        + tuple(shape(item.shape, BF16) for item in (cot_hbm, wq_hbm, wo_hbm)),
        (me, xf, xb, gain, frames, valid_counts, cot_hbm, wq_hbm, wo_hbm),
        scratch=(pltpu.VMEM(frames.shape, jnp.int32), pltpu.SMEM(valid_counts.shape, jnp.int32)),
        sems=(5,),
        smem=1,
        hbm=5,
    )
    pieces = gather_far(near, size)
    top, mix, stat, early, early_dp = call(
        attend_early,
        (
            shape((PAIRS, wide), F32),
            shape((PAIRS, HEAD_DIM + 16, wide), F32),
            shape((8, HEADS * rows), F32),
            shape((wide, HEADS * rows), BF16),
            shape((wide, HEADS * rows), F32),
        ),
        (pieces[0], pieces[-1], qf, qb, dout, bias),
    )
    layer_out = call(
        partial(attend_forward, size),
        shape((rows, width), BF16),
        (*pieces[1:-1], qf, bias, xf, wo, top, mix),
        scratch=(
            pltpu.VMEM((total, 2 * KV_COLS), BF16),
            pltpu.VMEM((2, total, wide), F32),
            pltpu.VMEM((HEADS * HEAD_DIM, rows), F32),
        ),
    )
    shifted = lax.ppermute(layer_out, "section", [((i - 1) % sections, i) for i in range(sections)])
    odd, *later = call(
        partial(attend_backward, size),
        (
            shape((half, rows, 2 * KV_COLS), BF16),
            shape((total, HEADS * rows), BF16),
            shape((total, HEADS * rows), BF16),
            spread,
            spread,
            shape((total, KV_COLS), BF16),
            shape((8, HEADS * rows), F32),
        ),
        (*pieces[1:-1], qb, dout, bias, pieces[0], pieces[-1], stat, early, early_dp),
        scratch=(
            pltpu.VMEM((total, KV_COLS), BF16),
            pltpu.VMEM((2, total, wide), F32),
            pltpu.VMEM((2, total, wide), F32),
            pltpu.VMEM((half * rows, 2 * KV_COLS), F32),
        ),
    )
    *even, dq = call(
        finish_backward,
        (kv_shape,) * half + (shape((rows, HEADS * HEAD_DIM), BF16),),
        later,
        scratch=(pltpu.VMEM((HEADS * HEAD_DIM, rows), F32),),
    )
    if by_permutes(size):
        other = swap(odd, 1, size)
        sums = call(partial(add_pieces, half), (kv_shape,) * half, (*even, other))
        received = [sums[-1]] + [swap(sums[i], 2 * i + 2, size) for i in range(half - 1)]
    else:
        both = jnp.stack([odd[i] for i in range(half)] + list(even)).astype(F32)
        places = jnp.argsort(jnp.array(order, jnp.int32) ^ lax.axis_index("seq"))
        summed = lax.psum_scatter(both[places], "seq", scatter_dimension=0, tiled=True)
        received = [summed[0].astype(BF16)]
    base, forward_next = call(
        query_back, (shape((rows, width), F32), shape((rows, width), BF16)), (dq, wq, shifted), sems=(), out_hbm=1
    )
    input_grad = call(
        partial(input_back, len(received)), shape((rows, width), BF16), (*received, base, xb, cot, gain, wkv)
    )
    backward_next = lax.ppermute(input_grad, "section", [((i + 1) % sections, i) for i in range(sections)])
    return (forward_next[None], backward_next[None])


def placed(size, *arrays):
    return on_device(size, *arrays)


def solution(mesh):
    size = mesh.shape["seq"]
    return jax.shard_map(
        partial(placed, size),
        mesh=mesh,
        in_specs=(
            P("section", "seq", None),
            P("section", "seq", None),
            P("section", "seq", None),
            P("section", None),
            P("section", None, None),
            P("section", None, None),
            P("section", None, None),
            P("section", None, None),
            P(),
            P(),
        ),
        out_specs=(P("section", "seq", None), P("section", "seq", None)),
        check_vma=False,
    )
```

```python
from functools import partial
import math

import jax
import jax.numpy as jnp
from jax import lax
from jax.experimental import pallas as pl
from jax.experimental.pallas import tpu as pltpu
from jax.sharding import PartitionSpec as P


HEADS = 8
KV_HEADS = 2
HEAD_DIM = 64
GROUP = HEADS // KV_HEADS
KV_COLS = KV_HEADS * HEAD_DIM
PAIRS = HEADS // 2

NORM_EPSILON = 1e-05
MASKED_SCORE = -1e30

F32 = jnp.float32
BF16 = jnp.bfloat16

NN = (((1,), (0,)), ((), ()))
NT = (((1,), (1,)), ((), ()))


def dot(a, b, dims=NN):
    return lax.dot_general(a, b, dims, preferred_element_type=F32)


def vmem(count):
    return [pl.BlockSpec(memory_space=pltpu.VMEM)] * count


def shape(dims, dtype):
    return jax.ShapeDtypeStruct(dims, dtype)


def rms(inputs, gain):
    widened = inputs.astype(F32)
    inverse = lax.rsqrt(jnp.mean(widened * widened, axis=-1, keepdims=True) + NORM_EPSILON)
    return (widened * inverse * gain).astype(BF16), inverse, widened


def project_kv(gain_hbm, xf_hbm, xb_hbm, wk_hbm, wv_hbm, kv_ref, gain_ref, xf_ref, xb_ref, wkv_ref, sems):
    copies = [
        pltpu.make_async_copy(source, target, sems.at[place])
        for place, (source, target) in enumerate(
            (
                (xf_hbm, xf_ref),
                (gain_hbm, gain_ref),
                (xb_hbm, xb_ref),
                (wk_hbm, wkv_ref.at[:, :KV_COLS]),
                (wv_hbm, wkv_ref.at[:, KV_COLS:]),
            )
        )
    ]
    for copy in copies:
        copy.start()
    rows = xf_ref.shape[0]
    copies[0].wait()
    copies[1].wait()
    gain = gain_ref[...]
    normed_f, _, _ = rms(xf_ref[...], gain)
    copies[2].wait()
    normed_b, _, _ = rms(xb_ref[...], gain)
    normed = jnp.concatenate([normed_f, normed_b], axis=0)
    copies[3].wait()
    copies[4].wait()
    both = dot(normed, wkv_ref[...]).astype(BF16)
    kv_ref[:, : 2 * KV_COLS] = both[:rows]
    kv_ref[:, 2 * KV_COLS :] = both[rows:]


def spread_heads(flat, out_ref, scale):
    rows = flat.shape[0]
    flat = flat.astype(BF16).astype(F32) * scale
    lane = lax.broadcasted_iota(jnp.int32, (rows, KV_COLS), 1)
    for head in range(HEADS):
        tile = head // 2
        block = flat[:, tile * KV_COLS : (tile + 1) * KV_COLS]
        group = head // GROUP
        if head % 2 != group:
            block = pltpu.roll(block, HEAD_DIM, 1)
        block = jnp.where((lane // HEAD_DIM) == group, block, 0.0)
        out_ref[head * rows : (head + 1) * rows, :] = block.astype(BF16)


def prepare(
    order,
    me_ref,
    xf_ref,
    xb_ref,
    gain_ref,
    frames_hbm,
    counts_hbm,
    cot_hbm,
    wq_hbm,
    wo_hbm,
    qf_ref,
    qb_ref,
    dout_ref,
    bias_ref,
    cot_ref,
    wq_ref,
    wo_ref,
    frames_ref,
    counts_ref,
    sems,
):
    copies = [
        pltpu.make_async_copy(source, target, sems.at[place])
        for place, (source, target) in enumerate(
            (
                (wq_hbm, wq_ref),
                (frames_hbm, frames_ref),
                (counts_hbm, counts_ref),
                (cot_hbm, cot_ref),
                (wo_hbm, wo_ref),
            )
        )
    ]
    for copy in copies:
        copy.start()
    gain = gain_ref[...]
    rows = xf_ref.shape[0]
    normed_f, _, _ = rms(xf_ref[...], gain)
    normed_b, _, _ = rms(xb_ref[...], gain)
    copies[1].wait()
    copies[2].wait()
    me = me_ref[0]
    row = lax.broadcasted_iota(jnp.int32, (rows, rows), 0)
    query_frames = jnp.broadcast_to(frames_ref[pl.ds(me, 1), :], (rows, rows))
    for place, step in enumerate(order):
        source = jnp.bitwise_xor(me, step)
        own = jnp.broadcast_to(frames_ref[pl.ds(source, 1), :], (rows, rows))
        key_frames = jnp.transpose(own.astype(F32)).astype(jnp.int32)
        visible = (key_frames <= query_frames) & (row < counts_ref[source])
        bias_ref[place * rows : (place + 1) * rows, :] = jnp.where(visible, 0.0, MASKED_SCORE)
    scale = 1.0 / math.sqrt(HEAD_DIM)
    copies[0].wait()
    queries = dot(jnp.concatenate([normed_f, normed_b], axis=0), wq_ref[...])
    spread_heads(queries[:rows], qf_ref, scale)
    spread_heads(queries[rows:], qb_ref, scale)
    copies[3].wait()
    copies[4].wait()
    spread_heads(dot(cot_ref[...], wo_ref[...], NT), dout_ref, 1.0)


def plus(left, right):
    return right if left is None else left + right


def twice(bias):
    return jnp.concatenate([bias, bias], axis=1)


def score_block(keys, q_rows, bias):
    return dot(keys, q_rows, NT) + twice(bias)


def with_ones(values):
    values_t = jnp.transpose(values)
    ones = jnp.ones((16, values.shape[0]), BF16)
    return [
        jnp.concatenate([values_t[group * HEAD_DIM : (group + 1) * HEAD_DIM], ones], axis=0)
        for group in range(KV_HEADS)
    ]


def late_chunks(count, rows):
    half = count // 2
    odd = 3 if (half - 1) % 3 == 0 else 1
    even = 2 if half % 2 == 0 else 1
    blocks = [(start, odd) for start in range(1, half, odd)]
    blocks += [(start, even) for start in range(half, count - 2, even)]
    return [slice(start * rows, (start + pieces) * rows) for start, pieces in blocks]


def attend_early(
    far_ref, near_ref, own_ref, qf_ref, qb_ref, dout_ref, bias_ref, top_ref, mix_ref, stat_ref, e_ref, dp_ref
):
    rows = own_ref.shape[0]
    pieces = jnp.concatenate([far_ref[...], near_ref[...], own_ref[...]], axis=0)
    bias = jnp.concatenate([bias_ref[:rows, :], bias_ref[-2 * rows :, :]], axis=0)
    extended = with_ones(pieces[:, KV_COLS : 2 * KV_COLS])
    wide = 2 * rows
    blocks = {}
    for now in range(-1, PAIRS):
        ahead = now + 1
        if ahead < PAIRS:
            cols = slice(ahead * wide, (ahead + 1) * wide)
            prob_grad = dot(pieces[:, 3 * KV_COLS :], dout_ref[cols, :], NT)
            dp_ref[:, cols] = prob_grad
            blocks[ahead] = (
                score_block(pieces[:, :KV_COLS], qf_ref[cols, :], bias),
                score_block(pieces[:, 2 * KV_COLS : 3 * KV_COLS], qb_ref[cols, :], bias),
                prob_grad,
            )
        if now >= 0:
            cols = slice(now * wide, (now + 1) * wide)
            forward, backward, prob_grad = blocks[now]
            top = jnp.max(forward, axis=0, keepdims=True)
            top_ref[now : now + 1, :] = top
            mix_ref[now] = dot(extended[(2 * now) // GROUP], jnp.exp(forward - top).astype(BF16))
            top = jnp.max(backward, axis=0, keepdims=True)
            weights = jnp.exp(backward - top)
            stat_ref[0:1, cols] = top
            stat_ref[1:2, cols] = jnp.sum(weights, axis=0, keepdims=True)
            stat_ref[2:3, cols] = jnp.sum(weights * prob_grad, axis=0, keepdims=True)
            e_ref[:, cols] = weights.astype(BF16)


def attend_backward(count, *refs):
    pieces = refs[: count - 3]
    q_ref, dout_ref, bias_ref, far_ref, near_ref, own_ref, stat_ref, e1_ref, dp1_ref = refs[count - 3 : count + 6]
    odd_ref, u_ref, e_ref, qs_ref, ds_ref, keys_ref, rs_ref = refs[count + 6 : count + 13]
    values_ref, s_ref, dp_ref, acc_ref = refs[count + 13 :]
    rows = own_ref.shape[0]
    total = rows * count
    half = count // 2
    odd = slice(0, half * rows)
    for place, piece in enumerate((far_ref, *pieces, near_ref, own_ref)):
        lines = slice(place * rows, (place + 1) * rows)
        keys_ref[lines, :] = piece[:, 2 * KV_COLS : 3 * KV_COLS]
        values_ref[lines, :] = piece[:, 3 * KV_COLS :]
    scale = 1.0 / math.sqrt(HEAD_DIM)
    wide = 2 * rows
    chunks = late_chunks(count, rows)
    tops, stats, scaled = {}, {}, {}
    for step in range(-1, PAIRS + 1):
        ahead, now, behind = step + 1, step, step - 1
        top = row_sum = mixed = None
        for lines in chunks:
            if 0 <= now < PAIRS:
                cols = slice(now * wide, (now + 1) * wide)
                weights = jnp.exp(s_ref[now % 2, lines, :] - tops[now])
                prob_grad = dot(values_ref[lines, :], dout_ref[cols, :], NT)
                row_sum = plus(row_sum, jnp.sum(weights, axis=0, keepdims=True))
                mixed = plus(mixed, jnp.sum(weights * prob_grad, axis=0, keepdims=True))
                dp_ref[now % 2, lines, :] = prob_grad
                e_ref[lines, cols] = weights.astype(BF16)
            if ahead < PAIRS:
                q_rows = q_ref[ahead * wide : (ahead + 1) * wide, :]
                block = score_block(keys_ref[lines, :], q_rows, bias_ref[lines, :])
                s_ref[ahead % 2, lines, :] = block
                part = jnp.max(block, axis=0, keepdims=True)
                top = part if top is None else jnp.maximum(top, part)
            if behind >= 0:
                cols = slice(behind * wide, (behind + 1) * wide)
                difference = (dp_ref[behind % 2, lines, :] - stats[behind][0]).astype(BF16)
                u_ref[lines, cols] = e_ref[lines, cols] * difference
        if ahead < PAIRS:
            tops[ahead] = jnp.maximum(top, stat_ref[0:1, ahead * wide : (ahead + 1) * wide])
        if behind >= 0:
            cols = slice(behind * wide, (behind + 1) * wide)
            delta, factor = stats[behind]
            weights = e1_ref[:, cols].astype(F32) * factor
            score_grad = (weights * (dp1_ref[:, cols] - delta)).astype(BF16)
            weights = weights.astype(BF16)
            e_ref[:rows, cols] = weights[:rows]
            u_ref[:rows, cols] = score_grad[:rows]
            e_ref[total - 2 * rows :, cols] = weights[rows:]
            u_ref[total - 2 * rows :, cols] = score_grad[rows:]
            key_grad = dot(u_ref[odd, cols], scaled[behind][0])
            value_grad = dot(e_ref[odd, cols], scaled[behind][1])
            if behind:
                key_grad = key_grad + acc_ref[:, :KV_COLS]
                value_grad = value_grad + acc_ref[:, KV_COLS:]
            if behind < PAIRS - 1:
                acc_ref[:, :KV_COLS] = key_grad
                acc_ref[:, KV_COLS:] = value_grad
            else:
                for place in range(half):
                    inner = slice(place * rows, (place + 1) * rows)
                    odd_ref[place, :, :KV_COLS] = key_grad[inner].astype(BF16)
                    odd_ref[place, :, KV_COLS:] = value_grad[inner].astype(BF16)
        if 0 <= now < PAIRS:
            cols = slice(now * wide, (now + 1) * wide)
            factor = jnp.exp(stat_ref[0:1, cols] - tops[now])
            inverse_sum = 1.0 / (row_sum + factor * stat_ref[1:2, cols])
            stats[now] = ((mixed + factor * stat_ref[2:3, cols]) * inverse_sum, factor)
            rs_ref[0:1, cols] = inverse_sum * scale
            column = jnp.transpose(jnp.broadcast_to(inverse_sum, (KV_COLS, wide)))
            scaled[now] = (
                (q_ref[cols, :].astype(F32) * column).astype(BF16),
                (dout_ref[cols, :].astype(F32) * column).astype(BF16),
            )
            qs_ref[cols, :], ds_ref[cols, :] = scaled[now]


def finish_backward(u_ref, e_ref, qs_ref, ds_ref, keys_ref, rs_ref, *refs):
    even_refs, dq_ref, dqt_ref = refs[:-2], refs[-2], refs[-1]
    rows = even_refs[0].shape[0]
    even = slice(len(even_refs) * rows, 2 * len(even_refs) * rows)
    wide = 2 * rows
    key_grad = dot(u_ref[even, :], qs_ref[...]).astype(BF16)
    value_grad = dot(e_ref[even, :], ds_ref[...]).astype(BF16)
    for place, target in enumerate(even_refs):
        target[:, :KV_COLS] = key_grad[place * rows : (place + 1) * rows]
        target[:, KV_COLS:] = value_grad[place * rows : (place + 1) * rows]
    keys_t = jnp.transpose(keys_ref[...])
    for pair in range(PAIRS):
        group = (2 * pair) // GROUP
        cols = slice(pair * wide, (pair + 1) * wide)
        part = dot(keys_t[group * HEAD_DIM : (group + 1) * HEAD_DIM], u_ref[:, cols]) * rs_ref[0:1, cols]
        dqt_ref[2 * pair * HEAD_DIM : (2 * pair + 1) * HEAD_DIM, :] = part[:, :rows]
        dqt_ref[(2 * pair + 1) * HEAD_DIM : (2 * pair + 2) * HEAD_DIM, :] = part[:, rows:]
    dq_ref[...] = jnp.transpose(dqt_ref[...]).astype(BF16)


def attend_forward(count, *refs):
    pieces = refs[: count - 3]
    q_ref, bias_ref, x_ref, wo_ref, top_ref, mix_ref, out_ref = refs[count - 3 : count + 4]
    kv_ref, s_ref, at_ref = refs[count + 4 :]
    rows = pieces[0].shape[0]
    for place, piece in enumerate(pieces):
        kv_ref[(place + 1) * rows : (place + 2) * rows, :] = piece[:, : 2 * KV_COLS]
    chunks = late_chunks(count, rows)
    extended = [with_ones(kv_ref[lines, KV_COLS:]) for lines in chunks]
    wide = 2 * rows
    tops = {}
    for now in range(-1, PAIRS):
        ahead = now + 1
        top = mixed = None
        for place, lines in enumerate(chunks):
            if ahead < PAIRS:
                q_rows = q_ref[ahead * wide : (ahead + 1) * wide, :]
                block = score_block(kv_ref[lines, :KV_COLS], q_rows, bias_ref[lines, :])
                s_ref[ahead % 2, lines, :] = block
                part = jnp.max(block, axis=0, keepdims=True)
                top = part if top is None else jnp.maximum(top, part)
            if now >= 0:
                weights = jnp.exp(s_ref[now % 2, lines, :] - tops[now]).astype(BF16)
                mixed = plus(mixed, dot(extended[place][(2 * now) // GROUP], weights))
        if ahead < PAIRS:
            tops[ahead] = jnp.maximum(top, top_ref[ahead : ahead + 1, :])
        if now >= 0:
            mixed = mixed + mix_ref[now] * jnp.exp(top_ref[now : now + 1, :] - tops[now])
            part = mixed[:HEAD_DIM] * (1.0 / mixed[HEAD_DIM : HEAD_DIM + 1])
            at_ref[2 * now * HEAD_DIM : (2 * now + 1) * HEAD_DIM, :] = part[:, :rows]
            at_ref[(2 * now + 1) * HEAD_DIM : (2 * now + 2) * HEAD_DIM, :] = part[:, rows:]
    attended = jnp.transpose(at_ref[...]).astype(BF16)
    out_ref[...] = (x_ref[...].astype(F32) + dot(attended, wo_ref[...])).astype(BF16)


def query_back(dq_ref, wq_ref, next_ref, out_ref, next_hbm, sem):
    copy = pltpu.make_async_copy(next_ref, next_hbm, sem)
    copy.start()
    out_ref[...] = dot(dq_ref[...], wq_ref[...], NT)
    copy.wait()


def add_pieces(steps, *refs):
    count = len(steps)
    for place, step in enumerate(steps):
        left = refs[place][...].astype(F32)
        refs[count + 1 + place][...] = (left + refs[count][step // 2].astype(F32)).astype(BF16)


def input_back(count, *refs):
    pieces = refs[:count]
    base_ref, x_ref, cot_ref, gain_ref, wkv_ref, out_ref = refs[count:]
    grads = pieces[0][...].astype(F32)
    for piece in pieces[1:]:
        grads = grads + piece[...].astype(F32)
    grads = grads.astype(BF16)
    gain = gain_ref[...]
    normed_grad = base_ref[...] + dot(grads, wkv_ref[...], NT)
    _, inverse, widened = rms(x_ref[...], gain)
    scaled = normed_grad * gain
    mean = jnp.mean(widened * scaled, axis=-1, keepdims=True)
    grad = cot_ref[...].astype(F32) + inverse * scaled - widened * (inverse * inverse * inverse * mean)
    out_ref[...] = grad.astype(BF16)


def local(array):
    return pltpu.with_memory_space_constraint(array, pltpu.VMEM)


def size_of(item):
    return math.prod(item.shape) * jnp.dtype(item.dtype).itemsize


def call(kernel, outs, args, scratch=(), sems=None, smem=0, hbm=0, out_hbm=0):
    many = isinstance(outs, (list, tuple))
    outs = list(outs) if many else [outs]
    inside, kept = len(args) - hbm, len(outs) - out_hbm
    args = list(args[:smem]) + [local(arg) for arg in args[smem:inside]] + [
        pltpu.with_memory_space_constraint(arg, pltpu.HBM) for arg in args[inside:]
    ]
    room = sum(size_of(item) for item in scratch) + (8 << 20)
    scratch = list(scratch) + ([] if sems is None else [pltpu.SemaphoreType.DMA(sems)])
    results = pl.pallas_call(
        kernel,
        out_shape=[pltpu.VMEM(out.shape, out.dtype) for out in outs[:kept]] + outs[kept:],
        in_specs=[pl.BlockSpec(memory_space=pltpu.SMEM)] * smem
        + vmem(inside - smem)
        + [pl.BlockSpec(memory_space=pltpu.HBM)] * hbm,
        out_specs=vmem(kept) + [pl.BlockSpec(memory_space=pltpu.HBM)] * out_hbm,
        scratch_shapes=scratch,
        compiler_params=pltpu.CompilerParams(vmem_limit_bytes=room),
    )(*args)
    return results if many else results[0]


def swap(block, step, size):
    return lax.ppermute(block, "seq", [(i, i ^ step) for i in range(size)])


def order_of(size):
    return list(range(1, size, 2)) + list(range(4, size, 2)) + [2, 0]


def by_permutes(size):
    return size == 8


def gather_near(block, size):
    if not by_permutes(size):
        return lax.all_gather(block, "seq", axis=0)
    return [block] + [swap(block, step, size) for step in range(2, size, 2)]


def gather_far(near, size):
    if not by_permutes(size):
        me = lax.axis_index("seq")
        return [lax.dynamic_index_in_dim(near, me ^ step, 0, False) for step in order_of(size)]
    far = [swap(piece, 1, size) for piece in near]
    return far + near[2:] + near[1:2] + near[:1]


def on_device(
    size,
    forward_input,
    stored_input,
    output_cotangent,
    norm_gain,
    query_weight,
    key_weight,
    value_weight,
    output_weight,
    frame_index,
    valid_counts,
):
    xf_hbm, xb_hbm, cot_hbm = forward_input[0], stored_input[0], output_cotangent[0]
    wq_hbm, wk_hbm, wv_hbm, wo_hbm = query_weight[0], key_weight[0], value_weight[0], output_weight[0]
    rows, width = xf_hbm.shape
    total = rows * size
    sections = lax.axis_size("section")
    order = order_of(size)
    half = size // 2
    kv_shape = shape((rows, 2 * KV_COLS), BF16)
    spread = shape((HEADS * rows, KV_COLS), BF16)
    wide = 2 * rows
    frames = frame_index.reshape(size, rows)
    me = lax.axis_index("seq").astype(jnp.int32).reshape(1)

    kv, gain, xf, xb, wkv = call(
        project_kv,
        (
            shape((rows, 4 * KV_COLS), BF16),
            shape(norm_gain.shape, F32),
            shape(xf_hbm.shape, BF16),
            shape(xb_hbm.shape, BF16),
            shape((width, 2 * KV_COLS), BF16),
        ),
        (norm_gain, xf_hbm, xb_hbm, wk_hbm, wv_hbm),
        sems=(5,),
        hbm=5,
    )
    near = gather_near(kv, size)
    qf, qb, dout, bias, cot, wq, wo = call(
        partial(prepare, order),
        (spread, spread, spread, shape((total, rows), F32))
        + tuple(shape(item.shape, BF16) for item in (cot_hbm, wq_hbm, wo_hbm)),
        (me, xf, xb, gain, frames, valid_counts, cot_hbm, wq_hbm, wo_hbm),
        scratch=(pltpu.VMEM(frames.shape, jnp.int32), pltpu.SMEM(valid_counts.shape, jnp.int32)),
        sems=(5,),
        smem=1,
        hbm=5,
    )
    pieces = gather_far(near, size)
    top, mix, stat, early, early_dp = call(
        attend_early,
        (
            shape((PAIRS, wide), F32),
            shape((PAIRS, HEAD_DIM + 16, wide), F32),
            shape((8, HEADS * rows), F32),
            shape((3 * rows, HEADS * rows), BF16),
            shape((3 * rows, HEADS * rows), F32),
        ),
        (pieces[0], *pieces[-2:], qf, qb, dout, bias),
    )
    layer_out = call(
        partial(attend_forward, size),
        shape((rows, width), BF16),
        (*pieces[1:-2], qf, bias, xf, wo, top, mix),
        scratch=(
            pltpu.VMEM((total, 2 * KV_COLS), BF16),
            pltpu.VMEM((2, total, wide), F32),
            pltpu.VMEM((HEADS * HEAD_DIM, rows), F32),
        ),
    )
    shifted = lax.ppermute(layer_out, "section", [((i - 1) % sections, i) for i in range(sections)])
    odd, *later = call(
        partial(attend_backward, size),
        (
            shape((half, rows, 2 * KV_COLS), BF16),
            shape((total, HEADS * rows), BF16),
            shape((total, HEADS * rows), BF16),
            spread,
            spread,
            shape((total, KV_COLS), BF16),
            shape((8, HEADS * rows), F32),
        ),
        (*pieces[1:-2], qb, dout, bias, pieces[0], *pieces[-2:], stat, early, early_dp),
        scratch=(
            pltpu.VMEM((total, KV_COLS), BF16),
            pltpu.VMEM((2, total, wide), F32),
            pltpu.VMEM((2, total, wide), F32),
            pltpu.VMEM((half * rows, 2 * KV_COLS), F32),
        ),
    )
    *even, dq = call(
        finish_backward,
        (kv_shape,) * half + (shape((rows, HEADS * HEAD_DIM), BF16),),
        later,
        scratch=(pltpu.VMEM((HEADS * HEAD_DIM, rows), F32),),
    )
    if by_permutes(size):
        other = swap(odd, 1, size)
        steps = order[half:]
        sums = call(partial(add_pieces, steps), (kv_shape,) * half, (*even, other))
        received = [sums[-1]] + [swap(sums[steps.index(step)], step, size) for step in sorted(steps)[1:]]
    else:
        both = jnp.stack([odd[i] for i in range(half)] + list(even)).astype(F32)
        places = jnp.argsort(jnp.array(order, jnp.int32) ^ lax.axis_index("seq"))
        summed = lax.psum_scatter(both[places], "seq", scatter_dimension=0, tiled=True)
        received = [summed[0].astype(BF16)]
    base, forward_next = call(
        query_back, (shape((rows, width), F32), shape((rows, width), BF16)), (dq, wq, shifted), sems=(), out_hbm=1
    )
    input_grad = call(
        partial(input_back, len(received)), shape((rows, width), BF16), (*received, base, xb, cot, gain, wkv)
    )
    backward_next = lax.ppermute(input_grad, "section", [((i + 1) % sections, i) for i in range(sections)])
    return (forward_next[None], backward_next[None])


def placed(size, *arrays):
    return on_device(size, *arrays)


def solution(mesh):
    size = mesh.shape["seq"]
    return jax.shard_map(
        partial(placed, size),
        mesh=mesh,
        in_specs=(
            P("section", "seq", None),
            P("section", "seq", None),
            P("section", "seq", None),
            P("section", None),
            P("section", None, None),
            P("section", None, None),
            P("section", None, None),
            P("section", None, None),
            P(),
            P(),
        ),
        out_specs=(P("section", "seq", None), P("section", "seq", None)),
        check_vma=False,
    )
```

```python
from functools import partial
import math

import jax
import jax.numpy as jnp
from jax import lax
from jax.experimental import pallas as pl
from jax.experimental.pallas import tpu as pltpu
from jax.sharding import PartitionSpec as P


HEADS = 8
KV_HEADS = 2
HEAD_DIM = 64
GROUP = HEADS // KV_HEADS
KV_COLS = KV_HEADS * HEAD_DIM
PAIRS = HEADS // 2

NORM_EPSILON = 1e-05
MASKED_SCORE = -1e30

F32 = jnp.float32
BF16 = jnp.bfloat16

NN = (((1,), (0,)), ((), ()))
NT = (((1,), (1,)), ((), ()))


def dot(a, b, dims=NN):
    return lax.dot_general(a, b, dims, preferred_element_type=F32)


def vmem(count):
    return [pl.BlockSpec(memory_space=pltpu.VMEM)] * count


def shape(dims, dtype):
    return jax.ShapeDtypeStruct(dims, dtype)


def rms(inputs, gain):
    widened = inputs.astype(F32)
    inverse = lax.rsqrt(jnp.mean(widened * widened, axis=-1, keepdims=True) + NORM_EPSILON)
    return (widened * inverse * gain).astype(BF16), inverse, widened


def project_kv(gain_hbm, xf_hbm, xb_hbm, wk_hbm, wv_hbm, kv_ref, gain_ref, xf_ref, xb_ref, wkv_ref, sems):
    copies = [
        pltpu.make_async_copy(source, target, sems.at[place])
        for place, (source, target) in enumerate(
            (
                (xf_hbm, xf_ref),
                (gain_hbm, gain_ref),
                (xb_hbm, xb_ref),
                (wk_hbm, wkv_ref.at[:, :KV_COLS]),
                (wv_hbm, wkv_ref.at[:, KV_COLS:]),
            )
        )
    ]
    for copy in copies:
        copy.start()
    rows = xf_ref.shape[0]
    copies[0].wait()
    copies[1].wait()
    gain = gain_ref[...]
    normed_f, _, _ = rms(xf_ref[...], gain)
    copies[2].wait()
    normed_b, _, _ = rms(xb_ref[...], gain)
    normed = jnp.concatenate([normed_f, normed_b], axis=0)
    copies[3].wait()
    copies[4].wait()
    both = dot(normed, wkv_ref[...]).astype(BF16)
    kv_ref[:, : 2 * KV_COLS] = both[:rows]
    kv_ref[:, 2 * KV_COLS :] = both[rows:]


def spread_heads(flat, out_ref, scale):
    rows = flat.shape[0]
    flat = flat.astype(BF16).astype(F32) * scale
    lane = lax.broadcasted_iota(jnp.int32, (rows, KV_COLS), 1)
    for head in range(HEADS):
        tile = head // 2
        block = flat[:, tile * KV_COLS : (tile + 1) * KV_COLS]
        group = head // GROUP
        if head % 2 != group:
            block = pltpu.roll(block, HEAD_DIM, 1)
        block = jnp.where((lane // HEAD_DIM) == group, block, 0.0)
        out_ref[head * rows : (head + 1) * rows, :] = block.astype(BF16)


def prepare(
    order,
    me_ref,
    xf_ref,
    xb_ref,
    gain_ref,
    frames_hbm,
    counts_hbm,
    cot_hbm,
    wq_hbm,
    wo_hbm,
    qf_ref,
    qb_ref,
    dout_ref,
    bias_ref,
    cot_ref,
    wq_ref,
    wo_ref,
    frames_ref,
    counts_ref,
    sems,
):
    copies = [
        pltpu.make_async_copy(source, target, sems.at[place])
        for place, (source, target) in enumerate(
            (
                (wq_hbm, wq_ref),
                (frames_hbm, frames_ref),
                (counts_hbm, counts_ref),
                (cot_hbm, cot_ref),
                (wo_hbm, wo_ref),
            )
        )
    ]
    for copy in copies:
        copy.start()
    gain = gain_ref[...]
    rows = xf_ref.shape[0]
    normed_f, _, _ = rms(xf_ref[...], gain)
    normed_b, _, _ = rms(xb_ref[...], gain)
    copies[1].wait()
    copies[2].wait()
    me = me_ref[0]
    row = lax.broadcasted_iota(jnp.int32, (rows, rows), 0)
    query_frames = jnp.broadcast_to(frames_ref[pl.ds(me, 1), :], (rows, rows))
    for place, step in enumerate(order):
        source = jnp.bitwise_xor(me, step)
        own = jnp.broadcast_to(frames_ref[pl.ds(source, 1), :], (rows, rows))
        key_frames = jnp.transpose(own.astype(F32)).astype(jnp.int32)
        visible = (key_frames <= query_frames) & (row < counts_ref[source])
        bias_ref[place * rows : (place + 1) * rows, :] = jnp.where(visible, 0.0, MASKED_SCORE)
    scale = 1.0 / math.sqrt(HEAD_DIM)
    copies[0].wait()
    queries = dot(jnp.concatenate([normed_f, normed_b], axis=0), wq_ref[...])
    spread_heads(queries[:rows], qf_ref, scale)
    spread_heads(queries[rows:], qb_ref, scale)
    copies[3].wait()
    copies[4].wait()
    spread_heads(dot(cot_ref[...], wo_ref[...], NT), dout_ref, 1.0)


def plus(left, right):
    return right if left is None else left + right


def twice(bias):
    return jnp.concatenate([bias, bias], axis=1)


def score_block(keys, q_rows, bias):
    return dot(keys, q_rows, NT) + twice(bias)


def with_ones(values):
    values_t = jnp.transpose(values)
    ones = jnp.ones((16, values.shape[0]), BF16)
    return [
        jnp.concatenate([values_t[group * HEAD_DIM : (group + 1) * HEAD_DIM], ones], axis=0)
        for group in range(KV_HEADS)
    ]


def late_chunks(count, rows):
    half = count // 2
    odd = 3 if (half - 1) % 3 == 0 else 1
    even = 2 if half % 2 == 0 else 1
    blocks = [(start, odd) for start in range(1, half, odd)]
    blocks += [(start, even) for start in range(half, count - 2, even)]
    return [slice(start * rows, (start + pieces) * rows) for start, pieces in blocks]


def attend_early(
    far_ref, near_ref, own_ref, qf_ref, qb_ref, dout_ref, bias_ref, top_ref, mix_ref, stat_ref, e_ref, dp_ref
):
    rows = own_ref.shape[0]
    pieces = jnp.concatenate([far_ref[...], near_ref[...], own_ref[...]], axis=0)
    bias = jnp.concatenate([bias_ref[:rows, :], bias_ref[-2 * rows :, :]], axis=0)
    extended = with_ones(pieces[:, KV_COLS : 2 * KV_COLS])
    wide = 2 * rows
    blocks = {}
    for now in range(-1, PAIRS):
        ahead = now + 1
        if ahead < PAIRS:
            cols = slice(ahead * wide, (ahead + 1) * wide)
            prob_grad = dot(pieces[:, 3 * KV_COLS :], dout_ref[cols, :], NT)
            dp_ref[:, cols] = prob_grad
            blocks[ahead] = (
                score_block(pieces[:, :KV_COLS], qf_ref[cols, :], bias),
                score_block(pieces[:, 2 * KV_COLS : 3 * KV_COLS], qb_ref[cols, :], bias),
                prob_grad,
            )
        if now >= 0:
            cols = slice(now * wide, (now + 1) * wide)
            forward, backward, prob_grad = blocks[now]
            top = jnp.max(forward, axis=0, keepdims=True)
            top_ref[now : now + 1, :] = top
            mix_ref[now] = dot(extended[(2 * now) // GROUP], jnp.exp(forward - top).astype(BF16))
            top = jnp.max(backward, axis=0, keepdims=True)
            weights = jnp.exp(backward - top)
            stat_ref[0:1, cols] = top
            stat_ref[1:2, cols] = jnp.sum(weights, axis=0, keepdims=True)
            stat_ref[2:3, cols] = jnp.sum(weights * prob_grad, axis=0, keepdims=True)
            e_ref[:, cols] = weights.astype(BF16)


def attend_late(count, *refs):
    late = count - 3
    pieces = refs[:late]
    qf_ref, x_ref, wo_ref, top_ref, mix_ref, qb_ref, dout_ref, bias_ref = refs[late : late + 8]
    far_ref, near_ref, own_ref, stat_ref, e1_ref, dp1_ref = refs[late + 8 : late + 14]
    out_ref, odd_ref, u_ref, e_ref, qs_ref, ds_ref, keys_ref, rs_ref = refs[late + 14 : late + 22]
    kv_ref, values_ref, s_ref, dp_ref, acc_ref, at_ref = refs[late + 22 :]
    rows = own_ref.shape[0]
    total = rows * count
    half = count // 2
    odd = slice(0, half * rows)
    wide = 2 * rows
    scale = 1.0 / math.sqrt(HEAD_DIM)
    chunks = late_chunks(count, rows)
    for place, piece in enumerate((far_ref, *pieces, near_ref, own_ref)):
        lines = slice(place * rows, (place + 1) * rows)
        kv_ref[lines, :] = piece[:, : 2 * KV_COLS]
        keys_ref[lines, :] = piece[:, 2 * KV_COLS : 3 * KV_COLS]
        values_ref[lines, :] = piece[:, 3 * KV_COLS :]
    extended = [with_ones(kv_ref[lines, KV_COLS:]) for lines in chunks]
    tops, stats, scaled = {}, {}, {}
    for step in range(-1, 2 * PAIRS + 1):
        ahead, now, behind = step + 1, step, step - 1
        pair = now % PAIRS
        cols = slice(pair * wide, (pair + 1) * wide)
        old = slice((behind % PAIRS) * wide, (behind % PAIRS + 1) * wide)
        new = slice((ahead % PAIRS) * wide, (ahead % PAIRS + 1) * wide)
        top = row_sum = mixed = None
        for place, lines in enumerate(chunks):
            if 0 <= now < PAIRS:
                weights = jnp.exp(s_ref[now % 2, lines, :] - tops[now]).astype(BF16)
                mixed = plus(mixed, dot(extended[place][(2 * pair) // GROUP], weights))
            elif PAIRS <= now < 2 * PAIRS:
                weights = jnp.exp(s_ref[now % 2, lines, :] - tops[now])
                prob_grad = dot(values_ref[lines, :], dout_ref[cols, :], NT)
                row_sum = plus(row_sum, jnp.sum(weights, axis=0, keepdims=True))
                mixed = plus(mixed, jnp.sum(weights * prob_grad, axis=0, keepdims=True))
                dp_ref[now % 2, lines, :] = prob_grad
                e_ref[lines, cols] = weights.astype(BF16)
            if ahead < 2 * PAIRS:
                keys = kv_ref[lines, :KV_COLS] if ahead < PAIRS else keys_ref[lines, :]
                q_rows = qf_ref[new, :] if ahead < PAIRS else qb_ref[new, :]
                block = score_block(keys, q_rows, bias_ref[lines, :])
                s_ref[ahead % 2, lines, :] = block
                part = jnp.max(block, axis=0, keepdims=True)
                top = part if top is None else jnp.maximum(top, part)
            if behind >= PAIRS:
                difference = (dp_ref[behind % 2, lines, :] - stats[behind][0]).astype(BF16)
                u_ref[lines, old] = e_ref[lines, old] * difference
        if ahead < PAIRS:
            tops[ahead] = jnp.maximum(top, top_ref[ahead : ahead + 1, :])
        elif ahead < 2 * PAIRS:
            tops[ahead] = jnp.maximum(top, stat_ref[0:1, new])
        if behind >= PAIRS:
            delta, factor = stats[behind]
            weights = e1_ref[:, old].astype(F32) * factor
            score_grad = (weights * (dp1_ref[:, old] - delta)).astype(BF16)
            weights = weights.astype(BF16)
            e_ref[:rows, old] = weights[:rows]
            u_ref[:rows, old] = score_grad[:rows]
            e_ref[total - 2 * rows :, old] = weights[rows:]
            u_ref[total - 2 * rows :, old] = score_grad[rows:]
            key_grad = dot(u_ref[odd, old], scaled[behind][0])
            value_grad = dot(e_ref[odd, old], scaled[behind][1])
            if behind > PAIRS:
                key_grad = key_grad + acc_ref[:, :KV_COLS]
                value_grad = value_grad + acc_ref[:, KV_COLS:]
            if behind < 2 * PAIRS - 1:
                acc_ref[:, :KV_COLS] = key_grad
                acc_ref[:, KV_COLS:] = value_grad
            else:
                for place in range(half):
                    inner = slice(place * rows, (place + 1) * rows)
                    odd_ref[place, :, :KV_COLS] = key_grad[inner].astype(BF16)
                    odd_ref[place, :, KV_COLS:] = value_grad[inner].astype(BF16)
        if 0 <= now < PAIRS:
            mixed = mixed + mix_ref[pair] * jnp.exp(top_ref[pair : pair + 1, :] - tops[now])
            part = mixed[:HEAD_DIM] * (1.0 / mixed[HEAD_DIM : HEAD_DIM + 1])
            at_ref[2 * pair * HEAD_DIM : (2 * pair + 1) * HEAD_DIM, :] = part[:, :rows]
            at_ref[(2 * pair + 1) * HEAD_DIM : (2 * pair + 2) * HEAD_DIM, :] = part[:, rows:]
        elif PAIRS <= now < 2 * PAIRS:
            factor = jnp.exp(stat_ref[0:1, cols] - tops[now])
            inverse_sum = 1.0 / (row_sum + factor * stat_ref[1:2, cols])
            stats[now] = ((mixed + factor * stat_ref[2:3, cols]) * inverse_sum, factor)
            rs_ref[0:1, cols] = inverse_sum * scale
            column = jnp.transpose(jnp.broadcast_to(inverse_sum, (KV_COLS, wide)))
            scaled[now] = (
                (qb_ref[cols, :].astype(F32) * column).astype(BF16),
                (dout_ref[cols, :].astype(F32) * column).astype(BF16),
            )
            qs_ref[cols, :], ds_ref[cols, :] = scaled[now]
        if now == PAIRS:
            attended = jnp.transpose(at_ref[...]).astype(BF16)
            out_ref[...] = (x_ref[...].astype(F32) + dot(attended, wo_ref[...])).astype(BF16)


def finish_backward(u_ref, e_ref, qs_ref, ds_ref, *even_refs):
    rows = even_refs[0].shape[0]
    even = slice(len(even_refs) * rows, 2 * len(even_refs) * rows)
    key_grad = dot(u_ref[even, :], qs_ref[...]).astype(BF16)
    value_grad = dot(e_ref[even, :], ds_ref[...]).astype(BF16)
    for place, target in enumerate(even_refs):
        target[:, :KV_COLS] = key_grad[place * rows : (place + 1) * rows]
        target[:, KV_COLS:] = value_grad[place * rows : (place + 1) * rows]


def query_back(u_ref, keys_ref, rs_ref, wq_ref, out_ref, dqt_ref):
    rows = out_ref.shape[0]
    wide = 2 * rows
    keys_t = jnp.transpose(keys_ref[...])
    for pair in range(PAIRS):
        group = (2 * pair) // GROUP
        cols = slice(pair * wide, (pair + 1) * wide)
        part = dot(keys_t[group * HEAD_DIM : (group + 1) * HEAD_DIM], u_ref[:, cols]) * rs_ref[0:1, cols]
        dqt_ref[2 * pair * HEAD_DIM : (2 * pair + 1) * HEAD_DIM, :] = part[:, :rows]
        dqt_ref[(2 * pair + 1) * HEAD_DIM : (2 * pair + 2) * HEAD_DIM, :] = part[:, rows:]
    query_grad = jnp.transpose(dqt_ref[...]).astype(BF16)
    out_ref[...] = dot(query_grad, wq_ref[...], NT)


def deliver(in_ref, out_hbm, sem):
    copy = pltpu.make_async_copy(in_ref, out_hbm, sem)
    copy.start()
    copy.wait()


def add_pieces(steps, *refs):
    count = len(steps)
    for place, step in enumerate(steps):
        left = refs[place][...].astype(F32)
        refs[count + 1 + place][...] = (left + refs[count][step // 2].astype(F32)).astype(BF16)


def input_back(count, *refs):
    pieces = refs[:count]
    base_ref, x_ref, cot_ref, gain_ref, wkv_ref, out_ref = refs[count:]
    grads = pieces[0][...].astype(F32)
    for piece in pieces[1:]:
        grads = grads + piece[...].astype(F32)
    grads = grads.astype(BF16)
    gain = gain_ref[...]
    normed_grad = base_ref[...] + dot(grads, wkv_ref[...], NT)
    _, inverse, widened = rms(x_ref[...], gain)
    scaled = normed_grad * gain
    mean = jnp.mean(widened * scaled, axis=-1, keepdims=True)
    grad = cot_ref[...].astype(F32) + inverse * scaled - widened * (inverse * inverse * inverse * mean)
    out_ref[...] = grad.astype(BF16)


def local(array):
    return pltpu.with_memory_space_constraint(array, pltpu.VMEM)


def size_of(item):
    return math.prod(item.shape) * jnp.dtype(item.dtype).itemsize


def call(kernel, outs, args, scratch=(), sems=None, smem=0, hbm=0, out_hbm=0):
    many = isinstance(outs, (list, tuple))
    outs = list(outs) if many else [outs]
    inside, kept = len(args) - hbm, len(outs) - out_hbm
    args = list(args[:smem]) + [local(arg) for arg in args[smem:inside]] + [
        pltpu.with_memory_space_constraint(arg, pltpu.HBM) for arg in args[inside:]
    ]
    room = sum(size_of(item) for item in scratch) + (8 << 20)
    scratch = list(scratch) + ([] if sems is None else [pltpu.SemaphoreType.DMA(sems)])
    results = pl.pallas_call(
        kernel,
        out_shape=[pltpu.VMEM(out.shape, out.dtype) for out in outs[:kept]] + outs[kept:],
        in_specs=[pl.BlockSpec(memory_space=pltpu.SMEM)] * smem
        + vmem(inside - smem)
        + [pl.BlockSpec(memory_space=pltpu.HBM)] * hbm,
        out_specs=vmem(kept) + [pl.BlockSpec(memory_space=pltpu.HBM)] * out_hbm,
        scratch_shapes=scratch,
        compiler_params=pltpu.CompilerParams(vmem_limit_bytes=room),
    )(*args)
    return results if many else results[0]


def swap(block, step, size):
    return lax.ppermute(block, "seq", [(i, i ^ step) for i in range(size)])


def order_of(size):
    return list(range(1, size, 2)) + list(range(4, size, 2)) + [2, 0]


def by_permutes(size):
    return size == 8


def gather_near(block, size):
    if not by_permutes(size):
        return lax.all_gather(block, "seq", axis=0)
    return [block] + [swap(block, step, size) for step in range(2, size, 2)]


def gather_far(near, size):
    if not by_permutes(size):
        me = lax.axis_index("seq")
        return [lax.dynamic_index_in_dim(near, me ^ step, 0, False) for step in order_of(size)]
    far = [swap(piece, 1, size) for piece in near]
    return far + near[2:] + near[1:2] + near[:1]


def on_device(
    size,
    forward_input,
    stored_input,
    output_cotangent,
    norm_gain,
    query_weight,
    key_weight,
    value_weight,
    output_weight,
    frame_index,
    valid_counts,
):
    xf_hbm, xb_hbm, cot_hbm = forward_input[0], stored_input[0], output_cotangent[0]
    wq_hbm, wk_hbm, wv_hbm, wo_hbm = query_weight[0], key_weight[0], value_weight[0], output_weight[0]
    rows, width = xf_hbm.shape
    total = rows * size
    sections = lax.axis_size("section")
    order = order_of(size)
    half = size // 2
    kv_shape = shape((rows, 2 * KV_COLS), BF16)
    spread = shape((HEADS * rows, KV_COLS), BF16)
    wide = 2 * rows
    frames = frame_index.reshape(size, rows)
    me = lax.axis_index("seq").astype(jnp.int32).reshape(1)

    kv, gain, xf, xb, wkv = call(
        project_kv,
        (
            shape((rows, 4 * KV_COLS), BF16),
            shape(norm_gain.shape, F32),
            shape(xf_hbm.shape, BF16),
            shape(xb_hbm.shape, BF16),
            shape((width, 2 * KV_COLS), BF16),
        ),
        (norm_gain, xf_hbm, xb_hbm, wk_hbm, wv_hbm),
        sems=(5,),
        hbm=5,
    )
    near = gather_near(kv, size)
    qf, qb, dout, bias, cot, wq, wo = call(
        partial(prepare, order),
        (spread, spread, spread, shape((total, rows), F32))
        + tuple(shape(item.shape, BF16) for item in (cot_hbm, wq_hbm, wo_hbm)),
        (me, xf, xb, gain, frames, valid_counts, cot_hbm, wq_hbm, wo_hbm),
        scratch=(pltpu.VMEM(frames.shape, jnp.int32), pltpu.SMEM(valid_counts.shape, jnp.int32)),
        sems=(5,),
        smem=1,
        hbm=5,
    )
    pieces = gather_far(near, size)
    top, mix, stat, early, early_dp = call(
        attend_early,
        (
            shape((PAIRS, wide), F32),
            shape((PAIRS, HEAD_DIM + 16, wide), F32),
            shape((8, HEADS * rows), F32),
            shape((3 * rows, HEADS * rows), BF16),
            shape((3 * rows, HEADS * rows), F32),
        ),
        (pieces[0], *pieces[-2:], qf, qb, dout, bias),
    )
    layer_out, odd, u, e, qs, ds, keys, rs = call(
        partial(attend_late, size),
        (
            shape((rows, width), BF16),
            shape((half, rows, 2 * KV_COLS), BF16),
            shape((total, HEADS * rows), BF16),
            shape((total, HEADS * rows), BF16),
            spread,
            spread,
            shape((total, KV_COLS), BF16),
            shape((8, HEADS * rows), F32),
        ),
        (
            *pieces[1:-2],
            *(qf, xf, wo, top, mix, qb, dout, bias),
            *(pieces[0], *pieces[-2:], stat, early, early_dp),
        ),
        scratch=(
            pltpu.VMEM((total, 2 * KV_COLS), BF16),
            pltpu.VMEM((total, KV_COLS), BF16),
            pltpu.VMEM((2, total, wide), F32),
            pltpu.VMEM((2, total, wide), F32),
            pltpu.VMEM((half * rows, 2 * KV_COLS), F32),
            pltpu.VMEM((HEADS * HEAD_DIM, rows), F32),
        ),
    )
    shifted = lax.ppermute(layer_out, "section", [((i - 1) % sections, i) for i in range(sections)])
    even = call(finish_backward, (kv_shape,) * half, (u, e, qs, ds))
    if by_permutes(size):
        other = swap(odd, 1, size)
        steps = order[half:]
        sums = call(partial(add_pieces, steps), (kv_shape,) * half, (*even, other))
        received = [sums[-1]] + [swap(sums[steps.index(step)], step, size) for step in sorted(steps)[1:]]
    else:
        both = jnp.stack([odd[i] for i in range(half)] + list(even)).astype(F32)
        places = jnp.argsort(jnp.array(order, jnp.int32) ^ lax.axis_index("seq"))
        summed = lax.psum_scatter(both[places], "seq", scatter_dimension=0, tiled=True)
        received = [summed[0].astype(BF16)]
    base = call(
        query_back, shape((rows, width), F32), (u, keys, rs, wq), scratch=(pltpu.VMEM((HEADS * HEAD_DIM, rows), F32),)
    )
    forward_next = call(deliver, shape((rows, width), BF16), (shifted,), sems=(), out_hbm=1)
    input_grad = call(
        partial(input_back, len(received)), shape((rows, width), BF16), (*received, base, xb, cot, gain, wkv)
    )
    backward_next = lax.ppermute(input_grad, "section", [((i + 1) % sections, i) for i in range(sections)])
    return (forward_next[None], backward_next[None])


def placed(size, *arrays):
    return on_device(size, *arrays)


def solution(mesh):
    size = mesh.shape["seq"]
    return jax.shard_map(
        partial(placed, size),
        mesh=mesh,
        in_specs=(
            P("section", "seq", None),
            P("section", "seq", None),
            P("section", "seq", None),
            P("section", None),
            P("section", None, None),
            P("section", None, None),
            P("section", None, None),
            P("section", None, None),
            P(),
            P(),
        ),
        out_specs=(P("section", "seq", None), P("section", "seq", None)),
        check_vma=False,
    )
```
